256 devices in a mesh: chan: 8 (over z), seqo: 4 (over y), seqi: 8 (over x, core).
Axes of the slice: x: 4, y: 4, z: 8, core: 2. Of those that a mesh axis runs over, the one named last changes fastest.
Arguments:
- gate_in: bfloat16 [65536, 4096], P(('seqo', 'seqi'), 'chan'), may hold values from -6 to 6
- value_in: bfloat16 [65536, 4096], P(('seqo', 'seqi'), 'chan'), may hold values from -6 to 6
- out_gate: bfloat16 [65536, 4096], P(('seqo', 'seqi'), 'chan'), may hold values from -6 to 6
- residual: bfloat16 [65536, 4096], P(('seqo', 'seqi'), 'chan'), may hold values from -200 to 200
- filters: bfloat16 [8, 32, 6, 65536], P('chan', ('seqo', 'seqi')), may hold values from -5 to 5
- kept_index: int32 [8, 128], P('chan'), may hold values from -1 to 511, as said below
- kept_owner: int32 [8, 128], P('chan'), may hold values from -1 to 31, as said below
- skip_bias: float32 [4096], P('chan'), may hold values from -1 to 1
- norm_gain: float32 [4096], P('chan'), may hold values from 0.5 to 1.5
Outputs:
- hidden_out: bfloat16 [65536, 4096], P(('seqo', 'seqi'), 'chan')
- normed: bfloat16 [65536, 4096], P(('seqo', 'seqi'), 'chan')
The draws below stay inside these ranges and needn't reach their ends.
Inputs may be any that keep to these rules, and one draw needn't show every extreme that they name: `kept_index`: row s lists the kept channels of slab s in rising order, distinct, between 64 and 128 of them, followed by -1 in the unused slots; some slab lists exactly 128. `kept_owner`: -1 exactly where kept_index is -1, else a device index along seqo+seqi. Within a slab no device owns more than 6 kept channels, and in every slab some device owns exactly 6.
All inputs are finite; a program needn't handle non-finite values.
Results may differ from the reference program's by a relative error of at most 0.005.
Values may be sent and summed in bfloat16 or wider, within the bound.
A program may use at most 128 MiB of HBM per device.

```python
import jax
import jax.numpy as jnp
from jax import lax

W = 4096
OWN_MAX = 6
SEQUENCE_LEN = 65536
SLAB = 512
KMAX = 128
N_CHAN = 8
N_SEQO = 4
N_SEQI = 8


def kept_lists(key):
    owner_count = N_SEQO * N_SEQI
    random_key_list = jax.random.split(jax.random.fold_in(key, 7001), 3)
    counts = jax.random.randint(random_key_list[0], (N_CHAN,), KMAX // 2, KMAX + 1)
    full_slab = jax.random.randint(random_key_list[1], (), 0, N_CHAN)
    counts = jnp.where(jnp.arange(N_CHAN) == full_slab, KMAX, counts)
    slab_keys = jax.random.split(random_key_list[2], N_CHAN)

    def one_slab(packed):
        slab_key, count = packed
        pieces = jax.random.split(slab_key, 5)
        slot_pos = jnp.arange(KMAX, dtype=jnp.int32)
        is_live = slot_pos < count
        chosen = jax.random.permutation(pieces[0], SLAB)[:KMAX]
        sorted_index = jnp.sort(jnp.where(is_live, chosen, SLAB))
        index_row = jnp.where(is_live, sorted_index, -1)
        owner_step = jax.random.randint(pieces[1], (owner_count,), 1, 4)
        heavy_owner = jax.random.randint(pieces[2], (), 0, owner_count)
        pair_owner = jnp.repeat(jnp.arange(owner_count, dtype=jnp.int32), OWN_MAX)
        pair_slot = jnp.tile(jnp.arange(OWN_MAX, dtype=jnp.int32), owner_count)
        pair_level = pair_slot // owner_step[pair_owner]
        pair_level = jnp.where(pair_owner == heavy_owner, -1, pair_level)
        pair_noise = jax.random.permutation(pieces[3], owner_count * OWN_MAX)
        priority = (pair_level + 1) * (owner_count * OWN_MAX) + pair_noise
        pair_order = jnp.argsort(priority, stable=True)
        picked = pair_owner[pair_order[:KMAX]]
        shuffle_key = jnp.where(is_live, jax.random.permutation(pieces[4], KMAX), KMAX + slot_pos)
        live_rank = jnp.argsort(jnp.argsort(shuffle_key, stable=True), stable=True)
        owners_row = jnp.where(is_live, picked[live_rank], -1)
        return (index_row.astype(jnp.int32), owners_row.astype(jnp.int32))
    return lax.map(one_slab, (slab_keys, counts))


def draw_kept_index(key, part):
    return kept_lists(key)[0].astype(jnp.int32)


def draw_kept_owner(key, part):
    return kept_lists(key)[1].astype(jnp.int32)


def draw_filters(key, part):
    owner_count = N_SEQO * N_SEQI
    random_key_list = jax.random.split(jax.random.fold_in(key, 7002), 6)
    array_shape = (N_CHAN, owner_count, OWN_MAX)
    slow_share = 0.5
    is_slow = jax.random.uniform(random_key_list[0], array_shape) < slow_share
    fast_rate = jnp.exp(jax.random.uniform(random_key_list[1], array_shape, minval=jnp.log(1.0 / 50.0), maxval=jnp.log(1.0 / 30.0)))
    slow_rate = jnp.exp(jax.random.uniform(random_key_list[2], array_shape, minval=jnp.log(0.05 / SEQUENCE_LEN), maxval=jnp.log(0.8 / SEQUENCE_LEN)))
    decay_rate = jnp.where(is_slow, slow_rate, fast_rate)
    floor_level = jnp.where(is_slow, 0.0, jnp.sqrt(1.0 / (2.0 * fast_rate * SEQUENCE_LEN)))
    spike_location = jax.random.randint(random_key_list[3], array_shape + (2,), 0, SEQUENCE_LEN)
    spike_retained = jax.random.uniform(random_key_list[4], array_shape + (2,), minval=0.5, maxval=0.8)
    token_position = jnp.arange(SEQUENCE_LEN, dtype=jnp.float32)
    decay_envelope = jnp.exp(-decay_rate[..., None] * token_position) + floor_level[..., None]
    for spike_number in range(2):
        passed_through = token_position >= spike_location[..., spike_number:spike_number + 1].astype(jnp.float32)
        decay_envelope = decay_envelope * jnp.where(passed_through, spike_retained[..., spike_number:spike_number + 1], 1.0)
    tap_values = jax.random.truncated_normal(random_key_list[5], -5.0, 5.0, array_shape + (SEQUENCE_LEN,)) * decay_envelope
    tap_scale = jnp.sqrt(jnp.sum(decay_envelope * decay_envelope, axis=-1, keepdims=True))
    return (tap_values / tap_scale).astype(jnp.bfloat16)


def draw_residual(key, part):
    random_key_list = jax.random.split(jax.random.fold_in(key, 7003), 1)
    column = jnp.arange(W, dtype=jnp.float32)
    column_rise = 1.0 + column / W
    standard = jax.random.truncated_normal(random_key_list[0], -6.0, 6.0, (SEQUENCE_LEN, W))
    values = standard * column_rise[None, :]
    return jnp.clip(values, -200.0, 200.0).astype(jnp.bfloat16)


def level_of(key, shape, cuts, smallest, largest):
    level = 1.0
    for axis_at, parts in cuts:
        draws = jax.random.uniform(jax.random.fold_in(jax.random.fold_in(key, 6), axis_at), (parts,), jnp.float32, smallest / len(cuts), largest / len(cuts))
        level = level * jnp.repeat(jnp.exp(draws), shape[axis_at] // parts).reshape((-1,) + (1,) * (len(shape) - 1 - axis_at))
    return level


def centred(key, extent, deviation, bound, shards=(), kind=jnp.bfloat16):
    loudness = level_of(key, extent, shards, -0.22, 0.18) if shards else 1.0
    drawn = jax.random.normal(key, extent, jnp.float32) * deviation * loudness
    return jnp.minimum(jnp.maximum(drawn, -bound), bound).astype(kind)


def setup_inputs(seed: int = 0) -> dict:
    arg_keys = jax.random.split(jax.random.key(seed), 10)
    gate_in = centred(arg_keys[0], (SEQUENCE_LEN, W), 1.0, 6.0, ((0, 32), (1, 8)))
    value_in = centred(arg_keys[1], (SEQUENCE_LEN, W), 1.0, 6.0, ((0, 32), (1, 8)))
    out_gate = centred(arg_keys[2], (SEQUENCE_LEN, W), 1.0, 6.0, ((0, 32), (1, 8)))
    residual = draw_residual(jax.random.fold_in(arg_keys[9], 71), 0)
    filters = draw_filters(jax.random.fold_in(arg_keys[9], 71), 0)
    kept_index = draw_kept_index(jax.random.fold_in(arg_keys[9], 71), 0)
    kept_owner = draw_kept_owner(jax.random.fold_in(arg_keys[9], 71), 0)
    skip_bias = jnp.clip(jax.random.uniform(arg_keys[7], (W,), jnp.float32, -1.0, 1.0) * level_of(arg_keys[7], (W,), ((0, 8),), -0.4, 0.0), -1.0, 1.0)
    norm_gain = jnp.clip(1.0 + 0.1 * jax.random.normal(arg_keys[8], (W,), jnp.float32), 0.5, 1.5)
    return {"gate_in": gate_in, "value_in": value_in, "out_gate": out_gate, "residual": residual, "filters": filters, "kept_index": kept_index, "kept_owner": kept_owner, "skip_bias": skip_bias, "norm_gain": norm_gain}


def owner_ranks(owners_row):
    is_live = owners_row >= 0
    slot_count = owners_row.shape[0]
    token_position = jnp.arange(slot_count, dtype=jnp.int32)
    earlier = (owners_row[:, None] == owners_row[None, :]) & is_live[None, :] & (token_position[None, :] < token_position[:, None])
    return lax.optimization_barrier(jnp.sum(earlier.astype(jnp.int32), axis=1)).astype(jnp.int32)

def slab_convolve(gated_slab, slab_filters, index_row, owners_row):
    is_live = owners_row >= 0
    slot_ranks = owner_ranks(owners_row)
    safe_owner = jnp.where(is_live, owners_row, 0).astype(jnp.int32)
    safe_rank = jnp.where(is_live, slot_ranks, 0).astype(jnp.int32)
    kernels = slab_filters[safe_owner, safe_rank].astype(jnp.float32)
    safe_index = jnp.where(is_live, index_row, 0).astype(jnp.int32)
    signals = jnp.take(gated_slab, safe_index, axis=1).T
    padded = 2 * SEQUENCE_LEN
    spectrum = jnp.fft.rfft(signals, n=padded, axis=1) * jnp.fft.rfft(kernels, n=padded, axis=1)
    causal = jnp.fft.irfft(spectrum, n=padded, axis=1)[:, :SEQUENCE_LEN]
    causal = jnp.where(is_live[:, None], causal, 0.0).astype(jnp.float32)
    target = jnp.where(is_live, index_row, SLAB).astype(jnp.int32)
    return jnp.zeros((SEQUENCE_LEN, SLAB), jnp.float32).at[:, target].set(causal.T, mode='drop')

def reference(gate_in, value_in, out_gate, residual, filters, kept_index, kept_owner, skip_bias, norm_gain):
    gated_prod = (gate_in.astype(jnp.float32) * value_in.astype(jnp.float32)).astype(jnp.bfloat16)
    gated_wide = gated_prod.astype(jnp.float32)
    slab_count = W // SLAB
    by_slab = gated_wide.reshape(SEQUENCE_LEN, slab_count, SLAB).transpose(1, 0, 2)
    convolved = lax.map(lambda packed: slab_convolve(*packed), (by_slab, filters, kept_index, kept_owner))
    convolved = convolved.transpose(1, 0, 2).reshape(SEQUENCE_LEN, W)
    mixed_out = out_gate.astype(jnp.float32) * (convolved + skip_bias[None, :] * gated_wide)
    hidden_out = (residual.astype(jnp.float32) + mixed_out).astype(jnp.bfloat16)
    hidden_wide = hidden_out.astype(jnp.float32)
    row_total = lax.optimization_barrier(jnp.sum(hidden_wide * hidden_wide, axis=1, keepdims=True))
    normed = (hidden_wide * lax.rsqrt(row_total / W + 1e-06) * norm_gain[None, :]).astype(jnp.bfloat16)
    return (hidden_out, normed)
```

```python
import functools

import jax
import jax.numpy as jnp
import numpy as np
from jax import lax
from jax.experimental import pallas as pl
from jax.experimental.pallas import tpu as pltpu
from jax.sharding import PartitionSpec as P

norm_eps = 1e-06
LANES = 128
MESH = pl.DeviceIdType.MESH
F32 = jnp.float32
BF16 = jnp.bfloat16


def split_table(table):
    high = table.astype(BF16)
    low = (table - high.astype(np.float64)).astype(BF16)
    return high, low


@functools.lru_cache(maxsize=None)
def tables(rows):
    step = np.arange(rows, dtype=np.float64) + 0.5
    outer = 2.0 * np.pi * np.outer(step, step) / (2 * rows)
    inner_at = np.arange(LANES, dtype=np.float64)
    twist = 2.0 * np.pi * np.outer(step, inner_at - LANES / 2) / (2 * rows * LANES)
    inner = 2.0 * np.pi * np.outer(inner_at, inner_at) / LANES
    outer_tab = np.stack([*split_table(np.cos(outer)), *split_table(-np.sin(outer))])
    twist_tab = np.stack([np.cos(twist), np.sin(twist)]).astype(np.float32)
    cos, sin = np.cos(inner), np.sin(inner)
    forward = np.block([[cos, -sin], [sin, cos]])
    back = np.block([[cos, sin], [-sin, cos]])
    inner_tab = np.stack([*split_table(forward), *split_table(back)])
    return outer_tab, twist_tab, inner_tab


def dot(a, b):
    return jnp.dot(a, b, preferred_element_type=F32)


def iota(shape, dim):
    return lax.broadcasted_iota(jnp.int32, shape, dim)


def main_kernel(
    slots,
    seqo,
    seqi,
    chan,
    index_ref,
    owner_ref,
    skip_ref,
    gate_hbm,
    value_hbm,
    og_hbm,
    res_hbm,
    filt_hbm,
    outer_hbm,
    twist_hbm,
    inner_hbm,
    hid_hbm,
    total_ref,
    gate,
    value,
    og,
    res,
    filt,
    outer,
    twist,
    inner,
    gated,
    base,
    hid,
    wide,
    fwide,
    sent,
    arrived,
    fpair,
    spec,
    turn_re,
    turn_im,
    back,
    ret,
    squares,
    parts,
    load_sem,
    local_sem,
    send_sem,
    recv_sem,
    bsend_sem,
    brecv_sem,
    zsend_sem,
    zrecv_sem,
    out_sem,
):
    owners = seqo * seqi
    pairs = slots // 2
    tok, width = gated.shape
    per = tok // LANES
    rows = per * owners
    live_slots = slots * owners
    me = lax.axis_index("seqo") * seqi + lax.axis_index("seqi")
    mez = lax.axis_index("chan")
    chunks = 4
    crow = tok // chunks
    tile = 256

    def load(src, dst, k):
        return pltpu.make_async_copy(src, dst, load_sem.at[k])

    def gate_loads(c):
        at = pl.ds(c * crow, crow)
        return (
            load(gate_hbm.at[at], gate.at[at], 2 * c),
            load(value_hbm.at[at], value.at[at], 2 * c + 1),
        )

    for c in range(chunks):
        for cp in gate_loads(c):
            cp.start()
    nl = 2 * chunks
    filt_load = load(filt_hbm.at[0, 0], filt, nl)
    outer_load = load(outer_hbm, outer, nl + 1)
    twist_load = load(twist_hbm, twist, nl + 2)
    inner_load = load(inner_hbm, inner, nl + 3)
    og_load = load(og_hbm, og, nl + 4)
    res_load = load(res_hbm, res, nl + 5)
    for cp in (filt_load, outer_load, twist_load, inner_load, og_load, res_load):
        cp.start()

    def plane(i):
        o = lax.rem(me + i, owners)
        return o, {"seqo": o // seqi, "seqi": lax.rem(o, seqi)}

    def column(i):
        return {"chan": lax.rem(mez + i, chan)}

    barrier = pltpu.get_barrier_semaphore()

    def greet_plane(i, carry):
        pl.semaphore_signal(barrier, inc=1, device_id=plane(i)[1], device_id_type=MESH)
        return carry

    def greet_column(i, carry):
        pl.semaphore_signal(barrier, inc=1, device_id=column(i), device_id_type=MESH)
        return carry

    lax.fori_loop(1, owners, greet_plane, 0)
    lax.fori_loop(1, chan, greet_column, 0)

    kmax = index_ref.shape[1]
    own_row = jnp.broadcast_to(owner_ref[...].astype(F32), (kmax, kmax))
    idx_row = jnp.broadcast_to(index_ref[...].astype(F32), (kmax, kmax))
    sub = iota((kmax, kmax), 0)
    lane = iota((kmax, kmax), 1)
    eye = sub == lane
    own_col = jnp.sum(jnp.where(eye, own_row, 0.0), axis=1, keepdims=True)
    idx_col = jnp.sum(jnp.where(eye, idx_row, 0.0), axis=1, keepdims=True)
    same = (jnp.broadcast_to(own_col, (kmax, kmax)) == own_row) & (sub < lane)
    rank = jnp.sum(jnp.where(same, 1.0, 0.0), axis=0, keepdims=True)
    own_one = owner_ref[...].astype(F32)
    slot_row = jnp.where(own_one >= 0.0, rank * owners + own_one, -1.0)
    slot_at = iota((live_slots, kmax), 0).astype(F32)
    select = jnp.where(slot_at == jnp.broadcast_to(slot_row, (live_slots, kmax)), 1.0, 0.0)
    chan_at = iota((kmax, width), 1).astype(F32)
    spread = jnp.where(chan_at == jnp.broadcast_to(idx_col, (kmax, width)), 1.0, 0.0)
    picker = dot(select.astype(BF16), spread.astype(BF16)).astype(BF16)

    for c in range(chunks):
        for cp in gate_loads(c):
            cp.wait()
        at = pl.ds(c * crow, crow)
        prod = (gate[at].astype(F32) * value[at].astype(F32)).astype(BF16)
        gated[at] = prod
        picked = lax.dot_general(
            picker, prod, (((1,), (1,)), ((), ())), preferred_element_type=F32
        )
        for q in range(crow // LANES):
            a = c * (crow // LANES) + q
            for r in range(slots):
                wide[r, pl.ds(a, owners, stride=per), :] = picked[
                    r * owners : (r + 1) * owners, q * LANES : (q + 1) * LANES
                ]

    def span(o):
        return pl.ds(pl.multiple_of(o * per, per), per)

    def exchange(p, src, dst, ssem, rsem):
        mine = pltpu.make_async_copy(
            src.at[p, span(me)], dst.at[p, span(me)], local_sem.at[0]
        )
        mine.start()

        def one(i, carry):
            o, dev = plane(i)
            pltpu.make_async_remote_copy(
                src_ref=src.at[p, span(o)],
                dst_ref=dst.at[p, span(me)],
                send_sem=ssem.at[p],
                recv_sem=rsem.at[p],
                device_id=dev,
                device_id_type=MESH,
            ).start()
            return carry

        lax.fori_loop(1, owners, one, 0)
        mine.wait()

    def whole(p, src, dst, ssem, rsem):
        most = pl.ds(0, rows - per)
        return pltpu.make_async_remote_copy(
            src_ref=src.at[p, most],
            dst_ref=dst.at[p, most],
            send_sem=ssem.at[p],
            recv_sem=rsem.at[p],
            device_id=plane(1)[1],
            device_id_type=MESH,
        )

    for p in range(pairs):
        for ch in range(2):
            sent[p, :, ch * LANES : (ch + 1) * LANES] = wide[2 * p + ch].astype(BF16)
        if p == 0:
            pl.semaphore_wait(barrier, owners + chan - 2)
        exchange(p, sent, arrived, send_sem, recv_sem)

    filt_load.wait()

    def unfold(a, carry):
        taps = filt[:, pl.ds(pl.multiple_of(a * LANES, LANES), LANES)].astype(F32)
        fwide[pl.ds(a, slots, stride=rows), :] = taps
        return carry

    lax.fori_loop(0, rows, unfold, 0, unroll=8)
    for r in range(slots):
        fpair[r // 2, :, (r % 2) * LANES : (r % 2 + 1) * LANES] = fwide[
            r * rows : (r + 1) * rows, :
        ].astype(BF16)

    outer_load.wait()
    twist_load.wait()
    inner_load.wait()

    def forward(x, at):
        re = dot(outer[0, at], x) + dot(outer[1, at], x)
        im = dot(outer[2, at], x) + dot(outer[3, at], x)
        tc, ts = twist[0, at], twist[1, at]
        out = []
        for ch in range(2):
            cut = slice(ch * LANES, (ch + 1) * LANES)
            r, m = re[:, cut], im[:, cut]
            z = jnp.concatenate([r * tc + m * ts, m * tc - r * ts], axis=1).astype(BF16)
            out.append(dot(z, inner[0]) + dot(z, inner[1]))
        return out

    scale = 1.0 / (rows * LANES)

    def filter_pair(p, carry):
        def step(k, carry):
            at = pl.ds(pl.multiple_of(k * tile, tile), tile)
            got = forward(fpair[p], at)
            for ch in range(2):
                spec[2 * p + ch, at] = got[ch] * scale
            return carry

        return lax.fori_loop(0, rows // tile, step, carry)

    lax.fori_loop(0, pairs, filter_pair, 0)

    def convolve_pair(p, carry):
        whole(p, sent, arrived, send_sem, recv_sem).wait_recv()

        def step(k, carry):
            at = pl.ds(pl.multiple_of(k * tile, tile), tile)
            got = forward(arrived[p], at)
            tc, ts = twist[0, at], twist[1, at]
            for ch in range(2):
                cut = slice(ch * LANES, (ch + 1) * LANES)
                kern = spec[2 * p + ch, at]
                sr, si = got[ch][:, :LANES], got[ch][:, LANES:]
                kr, ki = kern[:, :LANES], kern[:, LANES:]
                joint = jnp.concatenate([sr * kr - si * ki, sr * ki + si * kr], axis=1)
                joint = joint.astype(BF16)
                u = dot(joint, inner[2]) + dot(joint, inner[3])
                ur, ui = u[:, :LANES], u[:, LANES:]
                turn_re[at, cut] = (ur * tc - ui * ts).astype(BF16)
                turn_im[at, cut] = (ui * tc + ur * ts).astype(BF16)
            return carry

        lax.fori_loop(0, rows // tile, step, 0)

        def step_back(k, carry):
            at = pl.ds(pl.multiple_of(k * tile, tile), tile)
            u, v = turn_re[...], turn_im[...]
            y = (dot(outer[0, at], u) + dot(outer[1, at], u)) + (
                dot(outer[2, at], v) + dot(outer[3, at], v)
            )
            back[p, at] = y.astype(BF16)
            return carry

        lax.fori_loop(0, rows // tile, step_back, 0)
        exchange(p, back, ret, bsend_sem, brecv_sem)
        return carry

    lax.fori_loop(0, pairs, convolve_pair, 0)

    og_load.wait()
    res_load.wait()
    skip = skip_ref[...]

    def base_step(a, carry):
        at = pl.ds(pl.multiple_of(a * LANES, LANES), LANES)
        base[at] = res[at].astype(F32) + og[at].astype(F32) * (skip * gated[at].astype(F32))
        return carry

    lax.fori_loop(0, per, base_step, 0)

    for p in range(pairs):
        whole(p, back, ret, bsend_sem, brecv_sem).wait_recv()
        for ch in range(2):
            wide[2 * p + ch] = ret[p, :, ch * LANES : (ch + 1) * LANES].astype(F32)

    eye_tile = iota((LANES, LANES), 0) == iota((LANES, LANES), 1)

    def final_step(a, carry):
        at = pl.ds(pl.multiple_of(a * LANES, LANES), LANES)
        got = jnp.concatenate(
            [
                wide[r, pl.ds(a, owners, stride=per), :]
                for r in range(slots)
            ],
            axis=0,
        ).astype(BF16)
        conv = lax.dot_general(got, picker, (((0,), (0,)), ((), ())), preferred_element_type=F32)
        out = (base[at] + og[at].astype(F32) * conv).astype(BF16)
        hid[at] = out
        big = out.astype(F32)
        sq = big * big
        part = sq[:, :LANES]
        for j in range(1, width // LANES):
            part = part + sq[:, j * LANES : (j + 1) * LANES]
        row_sum = jnp.sum(part, axis=1, keepdims=True)
        line = jnp.where(eye_tile, jnp.broadcast_to(row_sum, (LANES, LANES)), 0.0)
        squares[pl.ds(a, 1), :] = jnp.sum(line, axis=0, keepdims=True)
        return carry

    lax.fori_loop(0, per, final_step, 0)
    hid_store = pltpu.make_async_copy(hid, hid_hbm, out_sem.at[0])
    hid_store.start()

    def send_sums(i, carry):
        pltpu.make_async_remote_copy(
            src_ref=squares,
            dst_ref=parts.at[i],
            send_sem=zsend_sem.at[i],
            recv_sem=zrecv_sem.at[i],
            device_id=column(i),
            device_id_type=MESH,
        ).start()
        return carry

    lax.fori_loop(1, chan, send_sums, 0)

    def take_sums(i, acc):
        cp = pltpu.make_async_remote_copy(
            src_ref=squares,
            dst_ref=parts.at[i],
            send_sem=zsend_sem.at[i],
            recv_sem=zrecv_sem.at[i],
            device_id=column(i),
            device_id_type=MESH,
        )
        cp.wait()
        return acc + parts[i]

    total_ref[...] = lax.fori_loop(1, chan, take_sums, squares[...])

    for p in range(pairs):
        whole(p, sent, arrived, send_sem, recv_sem).wait_send()
        whole(p, back, ret, bsend_sem, brecv_sem).wait_send()
    hid_store.wait()


def norm_kernel(width_all, hid_ref, total_ref, gain_ref, out_ref, normed_ref):
    groups = hid_ref.shape[0] // LANES
    eye_tile = iota((LANES, LANES), 0) == iota((LANES, LANES), 1)
    first = pl.program_id(0) * groups
    for a in range(groups):
        at = pl.ds(a * LANES, LANES)
        total = total_ref[pl.ds(first + a, 1), :]
        scaling = lax.rsqrt(total / width_all + norm_eps)
        line = jnp.where(eye_tile, jnp.broadcast_to(scaling, (LANES, LANES)), 0.0)
        col = jnp.sum(line, axis=1, keepdims=True)
        h = hid_ref[at]
        out_ref[at] = h
        normed_ref[at] = (h.astype(F32) * col * gain_ref[...]).astype(BF16)


def local(
    gate_in, value_in, out_gate, residual, filters, kept_index, kept_owner, skip_bias, norm_gain
):
    tok, width = gate_in.shape
    slots, length = filters.shape[2:]
    seqo, seqi, chan = (lax.axis_size(n) for n in ("seqo", "seqi", "chan"))
    owners = seqo * seqi
    per = tok // LANES
    rows = per * owners
    pairs = slots // 2
    outer_tab, twist_tab, inner_tab = tables(rows)
    vmem = pl.BlockSpec(memory_space=pltpu.VMEM)
    hbm = pl.BlockSpec(memory_space=pl.ANY)
    pair_shape = (pairs, rows, 2 * LANES)
    dma = pltpu.SemaphoreType.DMA
    hidden, total = pl.pallas_call(
        functools.partial(main_kernel, slots, seqo, seqi, chan),
        out_shape=(
            jax.ShapeDtypeStruct((tok, width), BF16),
            jax.ShapeDtypeStruct((per, LANES), F32),
        ),
        in_specs=[vmem] * 3 + [hbm] * 8,
        out_specs=(hbm, vmem),
        scratch_shapes=[
            pltpu.VMEM((tok, width), BF16),
            pltpu.VMEM((tok, width), BF16),
            pltpu.VMEM((tok, width), BF16),
            pltpu.VMEM((tok, width), BF16),
            pltpu.VMEM((slots, length), BF16),
            pltpu.VMEM(outer_tab.shape, BF16),
            pltpu.VMEM(twist_tab.shape, F32),
            pltpu.VMEM(inner_tab.shape, BF16),
            pltpu.VMEM((tok, width), BF16),
            pltpu.VMEM((tok, width), F32),
            pltpu.VMEM((tok, width), BF16),
            pltpu.VMEM((slots, rows, LANES), F32),
            pltpu.VMEM((slots * rows, LANES), F32),
            pltpu.VMEM(pair_shape, BF16),
            pltpu.VMEM(pair_shape, BF16),
            pltpu.VMEM(pair_shape, BF16),
            pltpu.VMEM((slots, rows, 2 * LANES), F32),
            pltpu.VMEM((rows, 2 * LANES), BF16),
            pltpu.VMEM((rows, 2 * LANES), BF16),
            pltpu.VMEM(pair_shape, BF16),
            pltpu.VMEM(pair_shape, BF16),
            pltpu.VMEM((per, LANES), F32),
            pltpu.VMEM((chan, per, LANES), F32),
            dma((14,)),
            dma((1,)),
            dma((pairs,)),
            dma((pairs,)),
            dma((pairs,)),
            dma((pairs,)),
            dma((chan,)),
            dma((chan,)),
            dma((1,)),
        ],
        compiler_params=pltpu.CompilerParams(
            collective_id=0, has_side_effects=True, vmem_limit_bytes=60 * 1024 * 1024
        ),
        name="hyena",
    )(
        kept_index,
        kept_owner,
        skip_bias.reshape(1, width),
        gate_in,
        value_in,
        out_gate,
        residual,
        filters,
        outer_tab,
        twist_tab,
        inner_tab,
    )
    block = tok // 4
    rows_spec = pl.BlockSpec((block, width), lambda i: (i, 0))
    return pl.pallas_call(
        functools.partial(norm_kernel, width * chan),
        grid=(4,),
        out_shape=(jax.ShapeDtypeStruct((tok, width), BF16),) * 2,
        in_specs=[
            rows_spec,
            pl.BlockSpec((per, LANES), lambda i: (0, 0)),
            pl.BlockSpec((1, width), lambda i: (0, 0)),
        ],
        out_specs=(rows_spec, rows_spec),
        name="norm",
    )(hidden, total, norm_gain.reshape(1, width))


def solution(mesh):
    by_token = P(("seqo", "seqi"), "chan")
    in_specs = (
        by_token,
        by_token,
        by_token,
        by_token,
        P("chan", ("seqo", "seqi"), None, None),
        P("chan", None),
        P("chan", None),
        P("chan"),
        P("chan"),
    )
    return jax.shard_map(
        local, mesh=mesh, in_specs=in_specs, out_specs=(by_token, by_token), check_vma=False
    )
```

```python
import functools

import jax
import jax.numpy as jnp
import numpy as np
from jax import lax
from jax.experimental import pallas as pl
from jax.experimental.pallas import tpu as pltpu
from jax.sharding import PartitionSpec as P

norm_eps = 1e-06
LANES = 128
MESH = pl.DeviceIdType.MESH
F32 = jnp.float32
BF16 = jnp.bfloat16


def split_table(table):
    high = table.astype(BF16)
    low = (table - high.astype(np.float64)).astype(BF16)
    return high, low


@functools.lru_cache(maxsize=None)
def tables(rows):
    step = np.arange(rows, dtype=np.float64) + 0.5
    outer = 2.0 * np.pi * np.outer(step, step) / (2 * rows)
    inner_at = np.arange(LANES, dtype=np.float64)
    twist = 2.0 * np.pi * np.outer(step, inner_at - LANES / 2) / (2 * rows * LANES)
    inner = 2.0 * np.pi * np.outer(inner_at, inner_at) / LANES
    outer_tab = np.stack([*split_table(np.cos(outer)), *split_table(-np.sin(outer))])
    twist_tab = np.stack([np.cos(twist), np.sin(twist)]).astype(np.float32)
    cos, sin = np.cos(inner), np.sin(inner)
    forward = np.block([[cos, -sin], [sin, cos]])
    back = np.block([[cos, sin], [-sin, cos]])
    inner_tab = np.stack([*split_table(forward), *split_table(back)])
    return outer_tab, twist_tab, inner_tab


def dot(a, b):
    return jnp.dot(a, b, preferred_element_type=F32)


def iota(shape, dim):
    return lax.broadcasted_iota(jnp.int32, shape, dim)


def main_kernel(
    slots,
    seqo,
    seqi,
    chan,
    index_ref,
    owner_ref,
    skip_ref,
    gate_hbm,
    value_hbm,
    og_hbm,
    res_hbm,
    filt_hbm,
    outer_hbm,
    twist_hbm,
    inner_hbm,
    hid_hbm,
    total_ref,
    gate,
    value,
    og,
    res,
    filt,
    outer,
    twist,
    inner,
    gated,
    hid,
    wide,
    wide_og,
    wide_base,
    fwide,
    sent,
    arrived,
    fpair,
    spec,
    turn_re,
    turn_im,
    back,
    ret,
    squares,
    parts,
    load_sem,
    local_sem,
    send_sem,
    recv_sem,
    bsend_sem,
    brecv_sem,
    zsend_sem,
    zrecv_sem,
    out_sem,
):
    owners = seqo * seqi
    pairs = slots // 2
    tok, width = gated.shape
    per = tok // LANES
    rows = per * owners
    live_slots = slots * owners
    me = lax.axis_index("seqo") * seqi + lax.axis_index("seqi")
    mez = lax.axis_index("chan")
    chunks = 4
    crow = tok // chunks
    tile = 256

    def load(src, dst, k):
        return pltpu.make_async_copy(src, dst, load_sem.at[k])

    def gate_loads(c):
        at = pl.ds(c * crow, crow)
        return (
            load(gate_hbm.at[at], gate.at[at], 2 * c),
            load(value_hbm.at[at], value.at[at], 2 * c + 1),
        )

    for c in range(chunks):
        for cp in gate_loads(c):
            cp.start()
    nl = 2 * chunks
    filt_load = load(filt_hbm.at[0, 0], filt, nl)
    outer_load = load(outer_hbm, outer, nl + 1)
    twist_load = load(twist_hbm, twist, nl + 2)
    inner_load = load(inner_hbm, inner, nl + 3)
    og_load = load(og_hbm, og, nl + 4)
    res_load = load(res_hbm, res, nl + 5)
    for cp in (filt_load, outer_load, twist_load, inner_load, og_load, res_load):
        cp.start()

    def plane(i):
        o = lax.rem(me + i, owners)
        return o, {"seqo": o // seqi, "seqi": lax.rem(o, seqi)}

    def partner(dy, dx, dc):
        y = lax.rem(lax.axis_index("seqo") + dy, seqo)
        i = lax.axis_index("seqi")
        x = lax.rem(i // 2 + dx, seqi // 2) * 2 + lax.rem(i + dc, 2)
        return y * seqi + x, {"seqo": y, "seqi": x}

    def ring(step, size):
        return min(step, size - step)

    steps = sorted(
        (
            (dy, dx, dc)
            for dy in range(seqo)
            for dx in range(seqi // 2)
            for dc in range(2)
            if dy or dx or dc
        ),
        key=lambda s: -ring(s[0], seqo) - ring(s[1], seqi // 2),
    )

    def column(i):
        return {"chan": lax.rem(mez + i, chan)}

    barrier = pltpu.get_barrier_semaphore()

    def greet_plane(i, carry):
        pl.semaphore_signal(barrier, inc=1, device_id=plane(i)[1], device_id_type=MESH)
        return carry

    def greet_column(i, carry):
        pl.semaphore_signal(barrier, inc=1, device_id=column(i), device_id_type=MESH)
        return carry

    lax.fori_loop(1, owners, greet_plane, 0)
    lax.fori_loop(1, chan, greet_column, 0)

    kmax = index_ref.shape[1]
    own_row = jnp.broadcast_to(owner_ref[...].astype(F32), (kmax, kmax))
    idx_row = jnp.broadcast_to(index_ref[...].astype(F32), (kmax, kmax))
    sub = iota((kmax, kmax), 0)
    lane = iota((kmax, kmax), 1)
    eye = sub == lane
    own_col = jnp.sum(jnp.where(eye, own_row, 0.0), axis=1, keepdims=True)
    idx_col = jnp.sum(jnp.where(eye, idx_row, 0.0), axis=1, keepdims=True)
    same = (jnp.broadcast_to(own_col, (kmax, kmax)) == own_row) & (sub < lane)
    rank = jnp.sum(jnp.where(same, 1.0, 0.0), axis=0, keepdims=True)
    own_one = owner_ref[...].astype(F32)
    slot_row = jnp.where(own_one >= 0.0, rank * owners + own_one, -1.0)
    slot_at = iota((live_slots, kmax), 0).astype(F32)
    select = jnp.where(slot_at == jnp.broadcast_to(slot_row, (live_slots, kmax)), 1.0, 0.0)
    chan_at = iota((kmax, width), 1).astype(F32)
    spread = jnp.where(chan_at == jnp.broadcast_to(idx_col, (kmax, width)), 1.0, 0.0)
    picker = dot(select.astype(BF16), spread.astype(BF16)).astype(BF16)

    def pick(x):
        return lax.dot_general(picker, x, (((1,), (1,)), ((), ())), preferred_element_type=F32)

    def lay_out(ref, picked, c):
        for q in range(crow // LANES):
            a = c * (crow // LANES) + q
            for r in range(slots):
                ref[r, pl.ds(a, owners, stride=per), :] = picked[
                    r * owners : (r + 1) * owners, q * LANES : (q + 1) * LANES
                ]

    for c in range(chunks):
        for cp in gate_loads(c):
            cp.wait()
        at = pl.ds(c * crow, crow)
        prod = (gate[at].astype(F32) * value[at].astype(F32)).astype(BF16)
        gated[at] = prod
        lay_out(wide, pick(prod), c)

    def span(o):
        return pl.ds(pl.multiple_of(o * per, per), per)

    def exchange(p, src, dst, ssem, rsem):
        mine = pltpu.make_async_copy(
            src.at[p, span(me)], dst.at[p, span(me)], local_sem.at[0]
        )
        mine.start()

        for step in steps:
            o, dev = partner(*step)
            pltpu.make_async_remote_copy(
                src_ref=src.at[p, span(o)],
                dst_ref=dst.at[p, span(me)],
                send_sem=ssem.at[p],
                recv_sem=rsem.at[p],
                device_id=dev,
                device_id_type=MESH,
            ).start()
        mine.wait()

    def whole(p, src, dst, ssem, rsem):
        most = pl.ds(0, rows - per)
        return pltpu.make_async_remote_copy(
            src_ref=src.at[p, most],
            dst_ref=dst.at[p, most],
            send_sem=ssem.at[p],
            recv_sem=rsem.at[p],
            device_id=plane(1)[1],
            device_id_type=MESH,
        )

    for p in range(pairs):
        for ch in range(2):
            sent[p, :, ch * LANES : (ch + 1) * LANES] = wide[2 * p + ch].astype(BF16)
        if p == 0:
            pl.semaphore_wait(barrier, owners + chan - 2)
        exchange(p, sent, arrived, send_sem, recv_sem)

    filt_load.wait()

    def unfold(a, carry):
        taps = filt[:, pl.ds(pl.multiple_of(a * LANES, LANES), LANES)].astype(F32)
        fwide[pl.ds(a, slots, stride=rows), :] = taps
        return carry

    lax.fori_loop(0, rows, unfold, 0, unroll=8)
    for r in range(slots):
        fpair[r // 2, :, (r % 2) * LANES : (r % 2 + 1) * LANES] = fwide[
            r * rows : (r + 1) * rows, :
        ].astype(BF16)

    outer_load.wait()
    twist_load.wait()
    inner_load.wait()

    def forward(x, at):
        re = dot(outer[0, at], x) + dot(outer[1, at], x)
        im = dot(outer[2, at], x) + dot(outer[3, at], x)
        tc, ts = twist[0, at], twist[1, at]
        out = []
        for ch in range(2):
            cut = slice(ch * LANES, (ch + 1) * LANES)
            r, m = re[:, cut], im[:, cut]
            z = jnp.concatenate([r * tc + m * ts, m * tc - r * ts], axis=1).astype(BF16)
            out.append(dot(z, inner[0]) + dot(z, inner[1]))
        return out

    scale = 1.0 / (rows * LANES)

    def filter_pair(p, carry):
        def step(k, carry):
            at = pl.ds(pl.multiple_of(k * tile, tile), tile)
            got = forward(fpair[p], at)
            for ch in range(2):
                spec[2 * p + ch, at] = got[ch] * scale
            return carry

        return lax.fori_loop(0, rows // tile, step, carry)

    lax.fori_loop(0, pairs, filter_pair, 0)

    def convolve_pair(p, carry):
        whole(p, sent, arrived, send_sem, recv_sem).wait_recv()

        def step(k, carry):
            at = pl.ds(pl.multiple_of(k * tile, tile), tile)
            got = forward(arrived[p], at)
            tc, ts = twist[0, at], twist[1, at]
            for ch in range(2):
                cut = slice(ch * LANES, (ch + 1) * LANES)
                kern = spec[2 * p + ch, at]
                sr, si = got[ch][:, :LANES], got[ch][:, LANES:]
                kr, ki = kern[:, :LANES], kern[:, LANES:]
                joint = jnp.concatenate([sr * kr - si * ki, sr * ki + si * kr], axis=1)
                joint = joint.astype(BF16)
                u = dot(joint, inner[2]) + dot(joint, inner[3])
                ur, ui = u[:, :LANES], u[:, LANES:]
                turn_re[at, cut] = (ur * tc - ui * ts).astype(BF16)
                turn_im[at, cut] = (ui * tc + ur * ts).astype(BF16)
            return carry

        lax.fori_loop(0, rows // tile, step, 0)

        def step_back(k, carry):
            at = pl.ds(pl.multiple_of(k * tile, tile), tile)
            u, v = turn_re[...], turn_im[...]
            y = (dot(outer[0, at], u) + dot(outer[1, at], u)) + (
                dot(outer[2, at], v) + dot(outer[3, at], v)
            )
            back[p, at] = y.astype(BF16)
            return carry

        lax.fori_loop(0, rows // tile, step_back, 0)
        exchange(p, back, ret, bsend_sem, brecv_sem)
        return carry

    lax.fori_loop(0, pairs, convolve_pair, 0)

    og_load.wait()
    res_load.wait()
    skip = skip_ref[...]
    picker_wide = picker.astype(F32)
    other = jnp.where(jnp.sum(picker_wide, axis=0, keepdims=True) > 0.0, 0.0, 1.0)
    skip_slot = jnp.sum(picker_wide * skip, axis=1, keepdims=True)

    for c in range(chunks):
        at = pl.ds(c * crow, crow)
        og_slot = pick(og[at])
        lay_out(wide_og, og_slot, c)
        base_slot = pick(res[at]) + og_slot * (skip_slot * pick(gated[at]))
        lay_out(wide_base, base_slot, c)

    eye_tile = iota((LANES, LANES), 0) == iota((LANES, LANES), 1)

    def rest_step(a, carry):
        at = pl.ds(pl.multiple_of(a * LANES, LANES), LANES)
        out = res[at].astype(F32) + og[at].astype(F32) * (skip * gated[at].astype(F32))
        out = (out * other).astype(BF16)
        hid[at] = out
        big = out.astype(F32)
        sq = big * big
        part = sq[:, :LANES]
        for j in range(1, width // LANES):
            part = part + sq[:, j * LANES : (j + 1) * LANES]
        row_sum = jnp.sum(part, axis=1, keepdims=True)
        line = jnp.where(eye_tile, jnp.broadcast_to(row_sum, (LANES, LANES)), 0.0)
        squares[pl.ds(a, 1), :] = jnp.sum(line, axis=0, keepdims=True)
        return carry

    lax.fori_loop(0, per, rest_step, 0, unroll=2)

    for p in range(pairs):
        whole(p, back, ret, bsend_sem, brecv_sem).wait_recv()
        for ch in range(2):
            r = 2 * p + ch

            def slot_step(o, acc):
                at = pl.ds(pl.multiple_of(o * per, per), per)
                conv = ret[p, at, ch * LANES : (ch + 1) * LANES].astype(F32)
                h = (wide_base[r, at] + wide_og[r, at] * conv).astype(BF16).astype(F32)
                wide[r, at] = h
                return acc + h * h

            squares[...] = lax.fori_loop(0, owners, slot_step, squares[...], unroll=8)

    def send_sums(i, carry):
        pltpu.make_async_remote_copy(
            src_ref=squares,
            dst_ref=parts.at[i],
            send_sem=zsend_sem.at[i],
            recv_sem=zrecv_sem.at[i],
            device_id=column(i),
            device_id_type=MESH,
        ).start()
        return carry

    lax.fori_loop(1, chan, send_sums, 0)

    def final_step(a, carry):
        at = pl.ds(pl.multiple_of(a * LANES, LANES), LANES)
        got = jnp.concatenate(
            [wide[r, pl.ds(a, owners, stride=per), :] for r in range(slots)],
            axis=0,
        ).astype(BF16)
        kept = lax.dot_general(got, picker, (((0,), (0,)), ((), ())), preferred_element_type=F32)
        hid[at] = (hid[at].astype(F32) + kept).astype(BF16)
        return carry

    lax.fori_loop(0, per, final_step, 0, unroll=4)
    hid_store = pltpu.make_async_copy(hid, hid_hbm, out_sem.at[0])
    hid_store.start()

    def take_sums(i, acc):
        cp = pltpu.make_async_remote_copy(
            src_ref=squares,
            dst_ref=parts.at[i],
            send_sem=zsend_sem.at[i],
            recv_sem=zrecv_sem.at[i],
            device_id=column(i),
            device_id_type=MESH,
        )
        cp.wait()
        return acc + parts[i]

    total_ref[...] = lax.fori_loop(1, chan, take_sums, squares[...])

    for p in range(pairs):
        whole(p, sent, arrived, send_sem, recv_sem).wait_send()
        whole(p, back, ret, bsend_sem, brecv_sem).wait_send()
    hid_store.wait()


def norm_kernel(width_all, hid_ref, total_ref, gain_ref, out_ref, normed_ref):
    groups = hid_ref.shape[0] // LANES
    eye_tile = iota((LANES, LANES), 0) == iota((LANES, LANES), 1)
    first = pl.program_id(0) * groups
    for a in range(groups):
        at = pl.ds(a * LANES, LANES)
        total = total_ref[pl.ds(first + a, 1), :]
        scaling = lax.rsqrt(total / width_all + norm_eps)
        line = jnp.where(eye_tile, jnp.broadcast_to(scaling, (LANES, LANES)), 0.0)
        col = jnp.sum(line, axis=1, keepdims=True)
        h = hid_ref[at]
        out_ref[at] = h
        normed_ref[at] = (h.astype(F32) * col * gain_ref[...]).astype(BF16)


def local(
    gate_in, value_in, out_gate, residual, filters, kept_index, kept_owner, skip_bias, norm_gain
):
    tok, width = gate_in.shape
    slots, length = filters.shape[2:]
    seqo, seqi, chan = (lax.axis_size(n) for n in ("seqo", "seqi", "chan"))
    owners = seqo * seqi
    per = tok // LANES
    rows = per * owners
    pairs = slots // 2
    outer_tab, twist_tab, inner_tab = tables(rows)
    vmem = pl.BlockSpec(memory_space=pltpu.VMEM)
    hbm = pl.BlockSpec(memory_space=pl.ANY)
    pair_shape = (pairs, rows, 2 * LANES)
    dma = pltpu.SemaphoreType.DMA
    hidden, total = pl.pallas_call(
        functools.partial(main_kernel, slots, seqo, seqi, chan),
        out_shape=(
            jax.ShapeDtypeStruct((tok, width), BF16),
            jax.ShapeDtypeStruct((per, LANES), F32),
        ),
        in_specs=[vmem] * 3 + [hbm] * 8,
        out_specs=(hbm, vmem),
        scratch_shapes=[
            pltpu.VMEM((tok, width), BF16),
            pltpu.VMEM((tok, width), BF16),
            pltpu.VMEM((tok, width), BF16),
            pltpu.VMEM((tok, width), BF16),
            pltpu.VMEM((slots, length), BF16),
            pltpu.VMEM(outer_tab.shape, BF16),
            pltpu.VMEM(twist_tab.shape, F32),
            pltpu.VMEM(inner_tab.shape, BF16),
            pltpu.VMEM((tok, width), BF16),
            pltpu.VMEM((tok, width), BF16),
            pltpu.VMEM((slots, rows, LANES), F32),
            pltpu.VMEM((slots, rows, LANES), F32),
            pltpu.VMEM((slots, rows, LANES), F32),
            pltpu.VMEM((slots * rows, LANES), F32),
            pltpu.VMEM(pair_shape, BF16),
            pltpu.VMEM(pair_shape, BF16),
            pltpu.VMEM(pair_shape, BF16),
            pltpu.VMEM((slots, rows, 2 * LANES), F32),
            pltpu.VMEM((rows, 2 * LANES), BF16),
            pltpu.VMEM((rows, 2 * LANES), BF16),
            pltpu.VMEM(pair_shape, BF16),
            pltpu.VMEM(pair_shape, BF16),
            pltpu.VMEM((per, LANES), F32),
            pltpu.VMEM((chan, per, LANES), F32),
            dma((14,)),
            dma((1,)),
            dma((pairs,)),
            dma((pairs,)),
            dma((pairs,)),
            dma((pairs,)),
            dma((chan,)),
            dma((chan,)),
            dma((1,)),
        ],
        compiler_params=pltpu.CompilerParams(
            collective_id=0, has_side_effects=True, vmem_limit_bytes=60 * 1024 * 1024
        ),
        name="hyena",
    )(
        kept_index,
        kept_owner,
        skip_bias.reshape(1, width),
        gate_in,
        value_in,
        out_gate,
        residual,
        filters,
        outer_tab,
        twist_tab,
        inner_tab,
    )
    block = tok // 4
    rows_spec = pl.BlockSpec((block, width), lambda i: (i, 0))
    return pl.pallas_call(
        functools.partial(norm_kernel, width * chan),
        grid=(4,),
        out_shape=(jax.ShapeDtypeStruct((tok, width), BF16),) * 2,
        in_specs=[
            rows_spec,
            pl.BlockSpec((per, LANES), lambda i: (0, 0)),
            pl.BlockSpec((1, width), lambda i: (0, 0)),
        ],
        out_specs=(rows_spec, rows_spec),
        name="norm",
    )(hidden, total, norm_gain.reshape(1, width))


def solution(mesh):
    by_token = P(("seqo", "seqi"), "chan")
    in_specs = (
        by_token,
        by_token,
        by_token,
        by_token,
        P("chan", ("seqo", "seqi"), None, None),
        P("chan", None),
        P("chan", None),
        P("chan"),
        P("chan"),
    )
    return jax.shard_map(
        local, mesh=mesh, in_specs=in_specs, out_specs=(by_token, by_token), check_vma=False
    )
```

```python
import functools

import jax
import jax.numpy as jnp
import numpy as np
from jax import lax
from jax.experimental import pallas as pl
from jax.experimental.pallas import tpu as pltpu
from jax.sharding import PartitionSpec as P

norm_eps = 1e-06
LANES = 128
MESH = pl.DeviceIdType.MESH
F32 = jnp.float32
BF16 = jnp.bfloat16


def split_table(table):
    high = table.astype(BF16)
    low = (table - high.astype(np.float64)).astype(BF16)
    return high, low


@functools.lru_cache(maxsize=None)
def tables(rows):
    step = np.arange(rows, dtype=np.float64) + 0.5
    outer = 2.0 * np.pi * np.outer(step, step) / (2 * rows)
    inner_at = np.arange(LANES, dtype=np.float64)
    twist = 2.0 * np.pi * np.outer(step, inner_at - LANES / 2) / (2 * rows * LANES)
    inner = 2.0 * np.pi * np.outer(inner_at, inner_at) / LANES
    outer_tab = np.stack([*split_table(np.cos(outer)), *split_table(-np.sin(outer))])
    twist_tab = np.stack([np.cos(twist), np.sin(twist)]).astype(np.float32)
    cos, sin = np.cos(inner), np.sin(inner)
    forward = np.block([[cos, -sin], [sin, cos]])
    back = np.block([[cos, sin], [-sin, cos]])
    inner_tab = np.stack([*split_table(forward), *split_table(back)])
    return outer_tab, twist_tab, inner_tab


def dot(a, b):
    return jnp.dot(a, b, preferred_element_type=F32)


def iota(shape, dim):
    return lax.broadcasted_iota(jnp.int32, shape, dim)


def main_kernel(
    slots,
    seqo,
    seqi,
    chan,
    index_ref,
    owner_ref,
    skip_ref,
    gate_hbm,
    value_hbm,
    og_hbm,
    res_hbm,
    filt_hbm,
    outer_hbm,
    twist_hbm,
    inner_hbm,
    hid,
    total_ref,
    gate,
    value,
    og,
    res,
    filt,
    outer,
    twist,
    inner,
    gated,
    wide,
    wide_og,
    wide_res,
    skip_slot,
    fwide,
    sent,
    arrived,
    fpair,
    spec,
    turn_re,
    turn_im,
    back,
    ret,
    squares,
    parts,
    load_sem,
    local_sem,
    send_sem,
    recv_sem,
    bsend_sem,
    brecv_sem,
    zsend_sem,
    zrecv_sem,
):
    owners = seqo * seqi
    pairs = slots // 2
    tok, width = gated.shape
    per = tok // LANES
    rows = per * owners
    live_slots = slots * owners
    me = lax.axis_index("seqo") * seqi + lax.axis_index("seqi")
    mez = lax.axis_index("chan")
    chunks = 4
    crow = tok // chunks
    tile = 256

    def load(src, dst, k):
        return pltpu.make_async_copy(src, dst, load_sem.at[k])

    def gate_loads(c):
        at = pl.ds(c * crow, crow)
        return (
            load(gate_hbm.at[at], gate.at[at], 2 * c),
            load(value_hbm.at[at], value.at[at], 2 * c + 1),
        )

    for c in range(chunks):
        for cp in gate_loads(c):
            cp.start()
    nl = 2 * chunks
    filt_load = load(filt_hbm.at[0, 0], filt, nl)
    outer_load = load(outer_hbm, outer, nl + 1)
    twist_load = load(twist_hbm, twist, nl + 2)
    inner_load = load(inner_hbm, inner, nl + 3)
    og_load = load(og_hbm, og, nl + 4)
    res_load = load(res_hbm, res, nl + 5)
    for cp in (filt_load, outer_load, twist_load, inner_load, og_load, res_load):
        cp.start()

    def plane(i):
        o = lax.rem(me + i, owners)
        return o, {"seqo": o // seqi, "seqi": lax.rem(o, seqi)}

    def partner(dy, dx, dc):
        y = lax.rem(lax.axis_index("seqo") + dy, seqo)
        i = lax.axis_index("seqi")
        x = lax.rem(i // 2 + dx, seqi // 2) * 2 + lax.rem(i + dc, 2)
        return y * seqi + x, {"seqo": y, "seqi": x}

    def ring(step, size):
        return min(step, size - step)

    steps = sorted(
        (
            (dy, dx, dc)
            for dy in range(seqo)
            for dx in range(seqi // 2)
            for dc in range(2)
            if dy or dx or dc
        ),
        key=lambda s: -ring(s[0], seqo) - ring(s[1], seqi // 2),
    )

    def column(i):
        return {"chan": lax.rem(mez + i, chan)}

    barrier = pltpu.get_barrier_semaphore()

    def greet_plane(i, carry):
        pl.semaphore_signal(barrier, inc=1, device_id=plane(i)[1], device_id_type=MESH)
        return carry

    def greet_column(i, carry):
        pl.semaphore_signal(barrier, inc=1, device_id=column(i), device_id_type=MESH)
        return carry

    lax.fori_loop(1, owners, greet_plane, 0)
    lax.fori_loop(1, chan, greet_column, 0)

    kmax = index_ref.shape[1]
    own_row = jnp.broadcast_to(owner_ref[...].astype(F32), (kmax, kmax))
    idx_row = jnp.broadcast_to(index_ref[...].astype(F32), (kmax, kmax))
    sub = iota((kmax, kmax), 0)
    lane = iota((kmax, kmax), 1)
    eye = sub == lane
    own_col = jnp.sum(jnp.where(eye, own_row, 0.0), axis=1, keepdims=True)
    idx_col = jnp.sum(jnp.where(eye, idx_row, 0.0), axis=1, keepdims=True)
    same = (jnp.broadcast_to(own_col, (kmax, kmax)) == own_row) & (sub < lane)
    rank = jnp.sum(jnp.where(same, 1.0, 0.0), axis=0, keepdims=True)
    own_one = owner_ref[...].astype(F32)
    slot_row = jnp.where(own_one >= 0.0, rank * owners + own_one, -1.0)
    slot_at = iota((live_slots, kmax), 0).astype(F32)
    select = jnp.where(slot_at == jnp.broadcast_to(slot_row, (live_slots, kmax)), 1.0, 0.0)
    chan_at = iota((kmax, width), 1).astype(F32)
    spread = jnp.where(chan_at == jnp.broadcast_to(idx_col, (kmax, width)), 1.0, 0.0)
    picker = dot(select.astype(BF16), spread.astype(BF16)).astype(BF16)

    def pick(x):
        return lax.dot_general(picker, x, (((1,), (1,)), ((), ())), preferred_element_type=F32)

    def lay_out(ref, picked, c):
        for q in range(crow // LANES):
            a = c * (crow // LANES) + q
            for r in range(slots):
                ref[r, pl.ds(a, owners, stride=per), :] = picked[
                    r * owners : (r + 1) * owners, q * LANES : (q + 1) * LANES
                ]

    for c in range(chunks):
        for cp in gate_loads(c):
            cp.wait()
        at = pl.ds(c * crow, crow)
        prod = (gate[at].astype(F32) * value[at].astype(F32)).astype(BF16)
        gated[at] = prod
        lay_out(wide, pick(prod), c)

    def span(o):
        return pl.ds(pl.multiple_of(o * per, per), per)

    def exchange(p, src, dst, ssem, rsem):
        mine = pltpu.make_async_copy(
            src.at[p, span(me)], dst.at[p, span(me)], local_sem.at[0]
        )
        mine.start()

        for step in steps:
            o, dev = partner(*step)
            pltpu.make_async_remote_copy(
                src_ref=src.at[p, span(o)],
                dst_ref=dst.at[p, span(me)],
                send_sem=ssem.at[p],
                recv_sem=rsem.at[p],
                device_id=dev,
                device_id_type=MESH,
            ).start()
        mine.wait()

    def whole(p, src, dst, ssem, rsem):
        most = pl.ds(0, rows - per)
        return pltpu.make_async_remote_copy(
            src_ref=src.at[p, most],
            dst_ref=dst.at[p, most],
            send_sem=ssem.at[p],
            recv_sem=rsem.at[p],
            device_id=plane(1)[1],
            device_id_type=MESH,
        )

    for p in range(pairs):
        for ch in range(2):
            sent[p, :, ch * LANES : (ch + 1) * LANES] = wide[2 * p + ch].astype(BF16)
        if p == 0:
            pl.semaphore_wait(barrier, owners + chan - 2)
        exchange(p, sent, arrived, send_sem, recv_sem)

    filt_load.wait()

    def unfold(a, carry):
        taps = filt[:, pl.ds(pl.multiple_of(a * LANES, LANES), LANES)].astype(F32)
        fwide[pl.ds(a, slots, stride=rows), :] = taps
        return carry

    lax.fori_loop(0, rows, unfold, 0, unroll=8)
    for r in range(slots):
        fpair[r // 2, :, (r % 2) * LANES : (r % 2 + 1) * LANES] = fwide[
            r * rows : (r + 1) * rows, :
        ].astype(BF16)

    outer_load.wait()
    twist_load.wait()
    inner_load.wait()

    def forward(x, at):
        re = dot(outer[0, at], x) + dot(outer[1, at], x)
        im = dot(outer[2, at], x) + dot(outer[3, at], x)
        tc, ts = twist[0, at], twist[1, at]
        out = []
        for ch in range(2):
            cut = slice(ch * LANES, (ch + 1) * LANES)
            r, m = re[:, cut], im[:, cut]
            z = jnp.concatenate([r * tc + m * ts, m * tc - r * ts], axis=1).astype(BF16)
            out.append(dot(z, inner[0]) + dot(z, inner[1]))
        return out

    scale = 1.0 / (rows * LANES)

    def filter_pair(p, carry):
        def step(k, carry):
            at = pl.ds(pl.multiple_of(k * tile, tile), tile)
            got = forward(fpair[p], at)
            for ch in range(2):
                spec[2 * p + ch, at] = got[ch] * scale
            return carry

        return lax.fori_loop(0, rows // tile, step, carry, unroll=2)

    lax.fori_loop(0, pairs, filter_pair, 0)

    def convolve_pair(p, carry):
        whole(p, sent, arrived, send_sem, recv_sem).wait_recv()

        def step(k, carry):
            at = pl.ds(pl.multiple_of(k * tile, tile), tile)
            got = forward(arrived[p], at)
            tc, ts = twist[0, at], twist[1, at]
            for ch in range(2):
                cut = slice(ch * LANES, (ch + 1) * LANES)
                kern = spec[2 * p + ch, at]
                sr, si = got[ch][:, :LANES], got[ch][:, LANES:]
                kr, ki = kern[:, :LANES], kern[:, LANES:]
                joint = jnp.concatenate([sr * kr - si * ki, sr * ki + si * kr], axis=1)
                joint = joint.astype(BF16)
                u = dot(joint, inner[2]) + dot(joint, inner[3])
                ur, ui = u[:, :LANES], u[:, LANES:]
                turn_re[at, cut] = (ur * tc - ui * ts).astype(BF16)
                turn_im[at, cut] = (ui * tc + ur * ts).astype(BF16)
            return carry

        lax.fori_loop(0, rows // tile, step, 0, unroll=2)

        def step_back(k, carry):
            at = pl.ds(pl.multiple_of(k * tile, tile), tile)
            u, v = turn_re[...], turn_im[...]
            y = (dot(outer[0, at], u) + dot(outer[1, at], u)) + (
                dot(outer[2, at], v) + dot(outer[3, at], v)
            )
            back[p, at] = y.astype(BF16)
            return carry

        lax.fori_loop(0, rows // tile, step_back, 0, unroll=2)
        exchange(p, back, ret, bsend_sem, brecv_sem)
        return carry

    lax.fori_loop(0, pairs, convolve_pair, 0)

    og_load.wait()
    res_load.wait()
    skip = skip_ref[...]
    picker_wide = picker.astype(F32)
    other = jnp.where(jnp.sum(picker_wide, axis=0, keepdims=True) > 0.0, 0.0, 1.0)
    skip_slot[...] = jnp.broadcast_to(
        jnp.sum(picker_wide * skip, axis=1, keepdims=True), skip_slot.shape
    )

    for c in range(chunks):
        at = pl.ds(c * crow, crow)
        lay_out(wide_og, pick(og[at]), c)
        lay_out(wide_res, pick(res[at]), c)

    eye_tile = iota((LANES, LANES), 0) == iota((LANES, LANES), 1)

    def rest_step(a, carry):
        at = pl.ds(pl.multiple_of(a * LANES, LANES), LANES)
        out = res[at].astype(F32) + og[at].astype(F32) * (skip * gated[at].astype(F32))
        out = (out * other).astype(BF16)
        hid[at] = out
        gram = lax.dot_general(out, out, (((1,), (1,)), ((), ())), preferred_element_type=F32)
        line = jnp.where(eye_tile, gram, 0.0)
        squares[pl.ds(a, 1), :] = jnp.sum(line, axis=0, keepdims=True)
        return carry

    lax.fori_loop(0, per, rest_step, 0, unroll=2)

    for p in range(pairs):
        whole(p, back, ret, bsend_sem, brecv_sem).wait_recv()
        for ch in range(2):
            r = 2 * p + ch

            def slot_step(o, acc):
                at = pl.ds(pl.multiple_of(o * per, per), per)
                conv = ret[p, at, ch * LANES : (ch + 1) * LANES].astype(F32)
                bias = skip_slot[pl.ds(r * owners + o, 1), :] * wide[r, at]
                h = (wide_res[r, at] + wide_og[r, at] * (conv + bias)).astype(BF16).astype(F32)
                wide[r, at] = h
                return acc + h * h

            squares[...] = lax.fori_loop(0, owners, slot_step, squares[...], unroll=8)

    def send_sums(i, carry):
        pltpu.make_async_remote_copy(
            src_ref=squares,
            dst_ref=parts.at[i],
            send_sem=zsend_sem.at[i],
            recv_sem=zrecv_sem.at[i],
            device_id=column(i),
            device_id_type=MESH,
        ).start()
        return carry

    lax.fori_loop(1, chan, send_sums, 0)

    def final_step(a, carry):
        at = pl.ds(pl.multiple_of(a * LANES, LANES), LANES)
        got = jnp.concatenate(
            [wide[r, pl.ds(a, owners, stride=per), :] for r in range(slots)],
            axis=0,
        ).astype(BF16)
        kept = lax.dot_general(got, picker, (((0,), (0,)), ((), ())), preferred_element_type=F32)
        hid[at] = (hid[at].astype(F32) + kept).astype(BF16)
        return carry

    lax.fori_loop(0, per, final_step, 0, unroll=4)

    def take_sums(i, acc):
        cp = pltpu.make_async_remote_copy(
            src_ref=squares,
            dst_ref=parts.at[i],
            send_sem=zsend_sem.at[i],
            recv_sem=zrecv_sem.at[i],
            device_id=column(i),
            device_id_type=MESH,
        )
        cp.wait()
        return acc + parts[i]

    total_ref[...] = lax.fori_loop(1, chan, take_sums, squares[...])

    for p in range(pairs):
        whole(p, sent, arrived, send_sem, recv_sem).wait_send()
        whole(p, back, ret, bsend_sem, brecv_sem).wait_send()


def norm_kernel(width_all, hid, total_ref, gain_ref, out_hbm, normed_hbm, normed, sem):
    keep = pltpu.make_async_copy(hid, out_hbm, sem.at[0])
    keep.start()
    tok = hid.shape[0]
    eye_tile = iota((LANES, LANES), 0) == iota((LANES, LANES), 1)
    block = 2 * LANES

    def store(b):
        at = pl.ds(b * block, block)
        return pltpu.make_async_copy(normed.at[at], normed_hbm.at[at], sem.at[b + 1])

    for b in range(tok // block):
        for a in range(b * block // LANES, (b + 1) * block // LANES):
            at = pl.ds(a * LANES, LANES)
            scaling = lax.rsqrt(total_ref[pl.ds(a, 1), :] / width_all + norm_eps)
            line = jnp.where(eye_tile, jnp.broadcast_to(scaling, (LANES, LANES)), 0.0)
            col = jnp.sum(line, axis=1, keepdims=True)
            normed[at] = (hid[at].astype(F32) * col * gain_ref[...]).astype(BF16)
        store(b).start()
    for b in range(tok // block):
        store(b).wait()
    keep.wait()


def local(
    gate_in, value_in, out_gate, residual, filters, kept_index, kept_owner, skip_bias, norm_gain
):
    tok, width = gate_in.shape
    slots, length = filters.shape[2:]
    seqo, seqi, chan = (lax.axis_size(n) for n in ("seqo", "seqi", "chan"))
    owners = seqo * seqi
    per = tok // LANES
    rows = per * owners
    pairs = slots // 2
    outer_tab, twist_tab, inner_tab = tables(rows)
    vmem = pl.BlockSpec(memory_space=pltpu.VMEM)
    hbm = pl.BlockSpec(memory_space=pl.ANY)
    pair_shape = (pairs, rows, 2 * LANES)
    dma = pltpu.SemaphoreType.DMA
    hidden, total = pl.pallas_call(
        functools.partial(main_kernel, slots, seqo, seqi, chan),
        out_shape=(
            pltpu.VMEM((tok, width), BF16),
            pltpu.VMEM((per, LANES), F32),
        ),
        in_specs=[vmem] * 3 + [hbm] * 8,
        out_specs=(vmem, vmem),
        scratch_shapes=[
            pltpu.VMEM((tok, width), BF16),
            pltpu.VMEM((tok, width), BF16),
            pltpu.VMEM((tok, width), BF16),
            pltpu.VMEM((tok, width), BF16),
            pltpu.VMEM((slots, length), BF16),
            pltpu.VMEM(outer_tab.shape, BF16),
            pltpu.VMEM(twist_tab.shape, F32),
            pltpu.VMEM(inner_tab.shape, BF16),
            pltpu.VMEM((tok, width), BF16),
            pltpu.VMEM((slots, rows, LANES), F32),
            pltpu.VMEM((slots, rows, LANES), F32),
            pltpu.VMEM((slots, rows, LANES), F32),
            pltpu.VMEM((slots * owners, LANES), F32),
            pltpu.VMEM((slots * rows, LANES), F32),
            pltpu.VMEM(pair_shape, BF16),
            pltpu.VMEM(pair_shape, BF16),
            pltpu.VMEM(pair_shape, BF16),
            pltpu.VMEM((slots, rows, 2 * LANES), F32),
            pltpu.VMEM((rows, 2 * LANES), BF16),
            pltpu.VMEM((rows, 2 * LANES), BF16),
            pltpu.VMEM(pair_shape, BF16),
            pltpu.VMEM(pair_shape, BF16),
            pltpu.VMEM((per, LANES), F32),
            pltpu.VMEM((chan, per, LANES), F32),
            dma((14,)),
            dma((1,)),
            dma((pairs,)),
            dma((pairs,)),
            dma((pairs,)),
            dma((pairs,)),
            dma((chan,)),
            dma((chan,)),
        ],
        compiler_params=pltpu.CompilerParams(
            collective_id=0, has_side_effects=True, vmem_limit_bytes=60 * 1024 * 1024
        ),
        name="hyena",
    )(
        kept_index,
        kept_owner,
        skip_bias.reshape(1, width),
        gate_in,
        value_in,
        out_gate,
        residual,
        filters,
        outer_tab,
        twist_tab,
        inner_tab,
    )
    return pl.pallas_call(
        functools.partial(norm_kernel, width * chan),
        out_shape=(jax.ShapeDtypeStruct((tok, width), BF16),) * 2,
        in_specs=[vmem] * 3,
        out_specs=(hbm, hbm),
        scratch_shapes=[pltpu.VMEM((tok, width), BF16), dma((tok // (2 * LANES) + 1,))],
        compiler_params=pltpu.CompilerParams(vmem_limit_bytes=8 * 1024 * 1024),
        name="norm",
    )(
        pltpu.with_memory_space_constraint(hidden, pltpu.VMEM),
        pltpu.with_memory_space_constraint(total, pltpu.VMEM),
        norm_gain.reshape(1, width),
    )


def solution(mesh):
    by_token = P(("seqo", "seqi"), "chan")
    in_specs = (
        by_token,
        by_token,
        by_token,
        by_token,
        P("chan", ("seqo", "seqi"), None, None),
        P("chan", None),
        P("chan", None),
        P("chan"),
        P("chan"),
    )
    return jax.shard_map(
        local, mesh=mesh, in_specs=in_specs, out_specs=(by_token, by_token), check_vma=False
    )
```

```python
import functools

import jax
import jax.numpy as jnp
import numpy as np
from jax import lax
from jax.experimental import pallas as pl
from jax.experimental.pallas import tpu as pltpu
from jax.sharding import PartitionSpec as P

norm_eps = 1e-06
LANES = 128
MESH = pl.DeviceIdType.MESH
F32 = jnp.float32
BF16 = jnp.bfloat16


def split_table(table):
    high = table.astype(BF16)
    low = (table - high.astype(np.float64)).astype(BF16)
    return high, low


@functools.lru_cache(maxsize=None)
def tables(rows):
    step = np.arange(rows, dtype=np.float64) + 0.5
    outer = 2.0 * np.pi * np.outer(step, step) / (2 * rows)
    inner_at = np.arange(LANES, dtype=np.float64)
    twist = 2.0 * np.pi * np.outer(step, inner_at - LANES / 2) / (2 * rows * LANES)
    inner = 2.0 * np.pi * np.outer(inner_at, inner_at) / LANES
    order = np.concatenate([np.arange(rows // 2), np.arange(rows - 1, rows // 2 - 1, -1)])
    cosine = np.cos(outer)[order]
    halves = [cosine[:, 0::2], cosine[:, 1::2]]
    outer_tab = np.stack([part for half in halves for part in split_table(half)])
    outer_back = np.stack([part for half in halves for part in split_table(half.T)])
    twist_tab = np.stack([np.cos(twist)[order], np.sin(twist)[order]]).astype(np.float32)
    cos, sin = np.cos(inner), np.sin(inner)
    forward = np.block([[cos, -sin], [sin, cos]])
    back = np.block([[cos, sin], [-sin, cos]])
    inner_tab = np.stack([*split_table(forward), *split_table(back)])
    return outer_tab, outer_back, twist_tab, inner_tab


def dot(a, b):
    return jnp.dot(a, b, preferred_element_type=F32)


def iota(shape, dim):
    return lax.broadcasted_iota(jnp.int32, shape, dim)


def main_kernel(
    slots,
    seqo,
    seqi,
    chan,
    index_ref,
    owner_ref,
    skip_ref,
    gate_hbm,
    value_hbm,
    og_hbm,
    res_hbm,
    filt_hbm,
    outer_hbm,
    outback_hbm,
    twist_hbm,
    inner_hbm,
    hid,
    total_ref,
    gate,
    value,
    og,
    res,
    filt,
    outer,
    outback,
    twist,
    inner,
    gated,
    wide,
    wide_og,
    wide_res,
    skip_slot,
    fwide,
    sent,
    arrived,
    fpair,
    spec,
    back,
    ret,
    squares,
    parts,
    load_sem,
    local_sem,
    send_sem,
    recv_sem,
    bsend_sem,
    brecv_sem,
    zsend_sem,
    zrecv_sem,
):
    owners = seqo * seqi
    pairs = slots // 2
    tok, width = gated.shape
    per = tok // LANES
    rows = per * owners
    live_slots = slots * owners
    me = lax.axis_index("seqo") * seqi + lax.axis_index("seqi")
    mez = lax.axis_index("chan")
    chunks = 4
    crow = tok // chunks

    def load(src, dst, k):
        return pltpu.make_async_copy(src, dst, load_sem.at[k])

    def gate_loads(c):
        at = pl.ds(c * crow, crow)
        return (
            load(gate_hbm.at[at], gate.at[at], 2 * c),
            load(value_hbm.at[at], value.at[at], 2 * c + 1),
        )

    for c in range(chunks):
        for cp in gate_loads(c):
            cp.start()
    nl = 2 * chunks
    filt_load = load(filt_hbm.at[0, 0], filt, nl)
    outer_load = load(outer_hbm, outer, nl + 1)
    twist_load = load(twist_hbm, twist, nl + 2)
    inner_load = load(inner_hbm, inner, nl + 3)
    og_load = load(og_hbm, og, nl + 4)
    res_load = load(res_hbm, res, nl + 5)
    outback_load = load(outback_hbm, outback, nl + 6)
    for cp in (filt_load, outer_load, twist_load, inner_load, outback_load, og_load, res_load):
        cp.start()

    def plane(i):
        o = lax.rem(me + i, owners)
        return o, {"seqo": o // seqi, "seqi": lax.rem(o, seqi)}

    def partner(dy, dx, dc):
        y = lax.rem(lax.axis_index("seqo") + dy, seqo)
        i = lax.axis_index("seqi")
        x = lax.rem(i // 2 + dx, seqi // 2) * 2 + lax.rem(i + dc, 2)
        return y * seqi + x, {"seqo": y, "seqi": x}

    def ring(step, size):
        return min(step, size - step)

    steps = sorted(
        (
            (dy, dx, dc)
            for dy in range(seqo)
            for dx in range(seqi // 2)
            for dc in range(2)
            if dy or dx or dc
        ),
        key=lambda s: -ring(s[0], seqo) - ring(s[1], seqi // 2),
    )

    def column(i):
        return {"chan": lax.rem(mez + i, chan)}

    barrier = pltpu.get_barrier_semaphore()

    def greet_plane(i, carry):
        pl.semaphore_signal(barrier, inc=1, device_id=plane(i)[1], device_id_type=MESH)
        return carry

    def greet_column(i, carry):
        pl.semaphore_signal(barrier, inc=1, device_id=column(i), device_id_type=MESH)
        return carry

    lax.fori_loop(1, owners, greet_plane, 0)
    lax.fori_loop(1, chan, greet_column, 0)

    kmax = index_ref.shape[1]
    own_row = jnp.broadcast_to(owner_ref[...].astype(F32), (kmax, kmax))
    idx_row = jnp.broadcast_to(index_ref[...].astype(F32), (kmax, kmax))
    sub = iota((kmax, kmax), 0)
    lane = iota((kmax, kmax), 1)
    eye = sub == lane
    own_col = jnp.sum(jnp.where(eye, own_row, 0.0), axis=1, keepdims=True)
    idx_col = jnp.sum(jnp.where(eye, idx_row, 0.0), axis=1, keepdims=True)
    same = (jnp.broadcast_to(own_col, (kmax, kmax)) == own_row) & (sub < lane)
    rank = jnp.sum(jnp.where(same, 1.0, 0.0), axis=0, keepdims=True)
    own_one = owner_ref[...].astype(F32)
    slot_row = jnp.where(own_one >= 0.0, rank * owners + own_one, -1.0)
    slot_at = iota((live_slots, kmax), 0).astype(F32)
    select = jnp.where(slot_at == jnp.broadcast_to(slot_row, (live_slots, kmax)), 1.0, 0.0)
    chan_at = iota((kmax, width), 1).astype(F32)
    spread = jnp.where(chan_at == jnp.broadcast_to(idx_col, (kmax, width)), 1.0, 0.0)
    picker = dot(select.astype(BF16), spread.astype(BF16)).astype(BF16)

    def place(a):
        return a % 2 * (per // 2) + a // 2

    def pick(x):
        return lax.dot_general(picker, x, (((1,), (1,)), ((), ())), preferred_element_type=F32)

    def lay_out(ref, picked, c):
        for q in range(crow // LANES):
            a = place(c * (crow // LANES) + q)
            for r in range(slots):
                ref[r, pl.ds(a, owners, stride=per), :] = picked[
                    r * owners : (r + 1) * owners, q * LANES : (q + 1) * LANES
                ]

    for c in range(chunks):
        for cp in gate_loads(c):
            cp.wait()
        at = pl.ds(c * crow, crow)
        prod = (gate[at].astype(F32) * value[at].astype(F32)).astype(BF16)
        gated[at] = prod
        lay_out(wide, pick(prod), c)

    def span(o):
        return pl.ds(pl.multiple_of(o * per, per), per)

    def exchange(p, src, dst, ssem, rsem):
        mine = pltpu.make_async_copy(
            src.at[p, span(me)], dst.at[p, span(me)], local_sem.at[0]
        )
        mine.start()

        for step in steps:
            o, dev = partner(*step)
            pltpu.make_async_remote_copy(
                src_ref=src.at[p, span(o)],
                dst_ref=dst.at[p, span(me)],
                send_sem=ssem.at[p],
                recv_sem=rsem.at[p],
                device_id=dev,
                device_id_type=MESH,
            ).start()
        mine.wait()

    def whole(p, src, dst, ssem, rsem):
        most = pl.ds(0, rows - per)
        return pltpu.make_async_remote_copy(
            src_ref=src.at[p, most],
            dst_ref=dst.at[p, most],
            send_sem=ssem.at[p],
            recv_sem=rsem.at[p],
            device_id=plane(1)[1],
            device_id_type=MESH,
        )

    for p in range(pairs):
        for ch in range(2):
            sent[p, :, ch * LANES : (ch + 1) * LANES] = wide[2 * p + ch].astype(BF16)
        if p == 0:
            pl.semaphore_wait(barrier, owners + chan - 2)
        exchange(p, sent, arrived, send_sem, recv_sem)

    filt_load.wait()

    half = rows // 2

    def unfold(m, carry):
        taps = filt[:, pl.ds(pl.multiple_of(m * 8 * LANES, 8 * LANES), 8 * LANES)].astype(F32)
        for i in range(8):
            at = pl.ds(i % 2 * half + i // 2 + 4 * m, slots, stride=rows)
            fwide[at, :] = taps[:, i * LANES : (i + 1) * LANES]
        return carry

    lax.fori_loop(0, rows // 8, unfold, 0, unroll=2)
    for r in range(slots):
        fpair[r // 2, :, (r % 2) * LANES : (r % 2 + 1) * LANES] = fwide[
            r * rows : (r + 1) * rows, :
        ].astype(BF16)

    outer_load.wait()
    twist_load.wait()
    inner_load.wait()
    outback_load.wait()

    def parity(x):
        groups = x.astype(F32).reshape(owners, 2, per // 2, 2 * LANES)
        return tuple(groups[:, i].reshape(half, 2 * LANES).astype(BF16) for i in range(2))

    def forward(even, odd):
        low, high = pl.ds(0, half), pl.ds(half, half)
        p = [dot(outer[0, at], even) + dot(outer[1, at], even) for at in (low, high)]
        q = [dot(outer[2, at], odd) + dot(outer[3, at], odd) for at in (low, high)]
        return [
            twisted(at, p[i] + q[i], q[1 - i] - p[1 - i]) for i, at in enumerate((low, high))
        ]

    def twisted(at, re, im):
        tc, ts = twist[0, at], twist[1, at]
        out = []
        for ch in range(2):
            cut = slice(ch * LANES, (ch + 1) * LANES)
            r, m = re[:, cut], im[:, cut]
            z = jnp.concatenate([r * tc + m * ts, m * tc - r * ts], axis=1).astype(BF16)
            out.append(dot(z, inner[0]) + dot(z, inner[1]))
        return out

    scale = 1.0 / (rows * LANES)

    def filter_pair(p, carry):
        got = forward(fpair[p, pl.ds(0, half)], fpair[p, pl.ds(half, half)])
        for i in range(2):
            for ch in range(2):
                spec[2 * p + ch, pl.ds(i * half, half)] = got[i][ch] * scale
        return carry

    lax.fori_loop(0, pairs, filter_pair, 0)

    def convolve_pair(p, carry):
        whole(p, sent, arrived, send_sem, recv_sem).wait_recv()
        got = forward(*parity(arrived[p]))
        turns = []
        for i in range(2):
            at = pl.ds(i * half, half)
            tc, ts = twist[0, at], twist[1, at]
            us, vs = [], []
            for ch in range(2):
                kern = spec[2 * p + ch, at]
                sr, si = got[i][ch][:, :LANES], got[i][ch][:, LANES:]
                kr, ki = kern[:, :LANES], kern[:, LANES:]
                joint = jnp.concatenate([sr * kr - si * ki, sr * ki + si * kr], axis=1)
                joint = joint.astype(BF16)
                u = dot(joint, inner[2]) + dot(joint, inner[3])
                ur, ui = u[:, :LANES], u[:, LANES:]
                us.append(ur * tc - ui * ts)
                vs.append(ui * tc + ur * ts)
            turns.append((jnp.concatenate(us, axis=1), jnp.concatenate(vs, axis=1)))
        halves = []
        for parity_at, sign in ((0, -1.0), (1, 1.0)):
            y = None
            for i in range(2):
                at = slice(i * half, (i + 1) * half)
                w = (turns[i][0] + sign * turns[1 - i][1]).astype(BF16)
                term = dot(outback[2 * parity_at, :, at], w) + dot(outback[2 * parity_at + 1, :, at], w)
                y = term if y is None else y + term
            halves.append(y.reshape(owners, 1, per // 2, 2 * LANES))
        back[p] = jnp.concatenate(halves, axis=1).reshape(rows, 2 * LANES).astype(BF16)
        exchange(p, back, ret, bsend_sem, brecv_sem)
        return carry

    lax.fori_loop(0, pairs, convolve_pair, 0)

    og_load.wait()
    res_load.wait()
    skip = skip_ref[...]
    picker_wide = picker.astype(F32)
    other = jnp.where(jnp.sum(picker_wide, axis=0, keepdims=True) > 0.0, 0.0, 1.0)
    skip_slot[...] = jnp.broadcast_to(
        jnp.sum(picker_wide * skip, axis=1, keepdims=True), skip_slot.shape
    )

    for c in range(chunks):
        at = pl.ds(c * crow, crow)
        lay_out(wide_og, pick(og[at]), c)
        lay_out(wide_res, pick(res[at]), c)

    eye_tile = iota((LANES, LANES), 0) == iota((LANES, LANES), 1)

    def rest_step(a, carry):
        at = pl.ds(pl.multiple_of(a * LANES, LANES), LANES)
        out = res[at].astype(F32) + og[at].astype(F32) * (skip * gated[at].astype(F32))
        out = (out * other).astype(BF16)
        hid[at] = out
        gram = lax.dot_general(out, out, (((1,), (1,)), ((), ())), preferred_element_type=F32)
        line = jnp.where(eye_tile, gram, 0.0)
        squares[pl.ds(place(a), 1), :] = jnp.sum(line, axis=0, keepdims=True)
        return carry

    lax.fori_loop(0, per, rest_step, 0, unroll=2)

    for p in range(pairs):
        whole(p, back, ret, bsend_sem, brecv_sem).wait_recv()
        for ch in range(2):
            r = 2 * p + ch

            def slot_step(o, acc):
                at = pl.ds(pl.multiple_of(o * per, per), per)
                conv = ret[p, at, ch * LANES : (ch + 1) * LANES].astype(F32)
                bias = skip_slot[pl.ds(r * owners + o, 1), :] * wide[r, at]
                h = (wide_res[r, at] + wide_og[r, at] * (conv + bias)).astype(BF16).astype(F32)
                wide[r, at] = h
                return acc + h * h

            squares[...] = lax.fori_loop(0, owners, slot_step, squares[...], unroll=8)

    def send_sums(i, carry):
        pltpu.make_async_remote_copy(
            src_ref=squares,
            dst_ref=parts.at[i],
            send_sem=zsend_sem.at[i],
            recv_sem=zrecv_sem.at[i],
            device_id=column(i),
            device_id_type=MESH,
        ).start()
        return carry

    lax.fori_loop(1, chan, send_sums, 0)

    def final_step(a, carry):
        at = pl.ds(pl.multiple_of(a * LANES, LANES), LANES)
        got = jnp.concatenate(
            [wide[r, pl.ds(place(a), owners, stride=per), :] for r in range(slots)],
            axis=0,
        ).astype(BF16)
        kept = lax.dot_general(got, picker, (((0,), (0,)), ((), ())), preferred_element_type=F32)
        hid[at] = (hid[at].astype(F32) + kept).astype(BF16)
        return carry

    lax.fori_loop(0, per, final_step, 0, unroll=4)

    def take_sums(i, acc):
        cp = pltpu.make_async_remote_copy(
            src_ref=squares,
            dst_ref=parts.at[i],
            send_sem=zsend_sem.at[i],
            recv_sem=zrecv_sem.at[i],
            device_id=column(i),
            device_id_type=MESH,
        )
        cp.wait()
        return acc + parts[i]

    total_ref[...] = lax.fori_loop(1, chan, take_sums, squares[...])

    for p in range(pairs):
        whole(p, sent, arrived, send_sem, recv_sem).wait_send()
        whole(p, back, ret, bsend_sem, brecv_sem).wait_send()


def norm_kernel(width_all, hid, total_ref, gain_ref, out_hbm, normed_hbm, normed, sem):
    keep = pltpu.make_async_copy(hid, out_hbm, sem.at[0])
    keep.start()
    tok = hid.shape[0]
    eye_tile = iota((LANES, LANES), 0) == iota((LANES, LANES), 1)
    block = 2 * LANES

    def store(b):
        at = pl.ds(b * block, block)
        return pltpu.make_async_copy(normed.at[at], normed_hbm.at[at], sem.at[b + 1])

    for b in range(tok // block):
        for a in range(b * block // LANES, (b + 1) * block // LANES):
            at = pl.ds(a * LANES, LANES)
            row = a % 2 * (tok // LANES // 2) + a // 2
            scaling = lax.rsqrt(total_ref[pl.ds(row, 1), :] / width_all + norm_eps)
            line = jnp.where(eye_tile, jnp.broadcast_to(scaling, (LANES, LANES)), 0.0)
            col = jnp.sum(line, axis=1, keepdims=True)
            normed[at] = (hid[at].astype(F32) * col * gain_ref[...]).astype(BF16)
        store(b).start()
    for b in range(tok // block):
        store(b).wait()
    keep.wait()


def local(
    gate_in, value_in, out_gate, residual, filters, kept_index, kept_owner, skip_bias, norm_gain
):
    tok, width = gate_in.shape
    slots, length = filters.shape[2:]
    seqo, seqi, chan = (lax.axis_size(n) for n in ("seqo", "seqi", "chan"))
    owners = seqo * seqi
    per = tok // LANES
    rows = per * owners
    pairs = slots // 2
    outer_tab, outer_back, twist_tab, inner_tab = tables(rows)
    vmem = pl.BlockSpec(memory_space=pltpu.VMEM)
    hbm = pl.BlockSpec(memory_space=pl.ANY)
    pair_shape = (pairs, rows, 2 * LANES)
    dma = pltpu.SemaphoreType.DMA
    hidden, total = pl.pallas_call(
        functools.partial(main_kernel, slots, seqo, seqi, chan),
        out_shape=(
            pltpu.VMEM((tok, width), BF16),
            pltpu.VMEM((per, LANES), F32),
        ),
        in_specs=[vmem] * 3 + [hbm] * 9,
        out_specs=(vmem, vmem),
        scratch_shapes=[
            pltpu.VMEM((tok, width), BF16),
            pltpu.VMEM((tok, width), BF16),
            pltpu.VMEM((tok, width), BF16),
            pltpu.VMEM((tok, width), BF16),
            pltpu.VMEM((slots, length), BF16),
            pltpu.VMEM(outer_tab.shape, BF16),
            pltpu.VMEM(outer_back.shape, BF16),
            pltpu.VMEM(twist_tab.shape, F32),
            pltpu.VMEM(inner_tab.shape, BF16),
            pltpu.VMEM((tok, width), BF16),
            pltpu.VMEM((slots, rows, LANES), F32),
            pltpu.VMEM((slots, rows, LANES), F32),
            pltpu.VMEM((slots, rows, LANES), F32),
            pltpu.VMEM((slots * owners, LANES), F32),
            pltpu.VMEM((8 * rows, LANES), F32),
            pltpu.VMEM(pair_shape, BF16),
            pltpu.VMEM(pair_shape, BF16),
            pltpu.VMEM(pair_shape, BF16),
            pltpu.VMEM((slots, rows, 2 * LANES), F32),
            pltpu.VMEM(pair_shape, BF16),
            pltpu.VMEM(pair_shape, BF16),
            pltpu.VMEM((per, LANES), F32),
            pltpu.VMEM((chan, per, LANES), F32),
            dma((15,)),
            dma((1,)),
            dma((pairs,)),
            dma((pairs,)),
            dma((pairs,)),
            dma((pairs,)),
            dma((chan,)),
            dma((chan,)),
        ],
        compiler_params=pltpu.CompilerParams(
            collective_id=0, has_side_effects=True, vmem_limit_bytes=60 * 1024 * 1024
        ),
        name="hyena",
    )(
        kept_index,
        kept_owner,
        skip_bias.reshape(1, width),
        gate_in,
        value_in,
        out_gate,
        residual,
        filters,
        outer_tab,
        outer_back,
        twist_tab,
        inner_tab,
    )
    return pl.pallas_call(
        functools.partial(norm_kernel, width * chan),
        out_shape=(jax.ShapeDtypeStruct((tok, width), BF16),) * 2,
        in_specs=[vmem] * 3,
        out_specs=(hbm, hbm),
        scratch_shapes=[pltpu.VMEM((tok, width), BF16), dma((tok // (2 * LANES) + 1,))],
        compiler_params=pltpu.CompilerParams(vmem_limit_bytes=8 * 1024 * 1024),
        name="norm",
    )(
        pltpu.with_memory_space_constraint(hidden, pltpu.VMEM),
        pltpu.with_memory_space_constraint(total, pltpu.VMEM),
        norm_gain.reshape(1, width),
    )


def solution(mesh):
    by_token = P(("seqo", "seqi"), "chan")
    in_specs = (
        by_token,
        by_token,
        by_token,
        by_token,
        P("chan", ("seqo", "seqi"), None, None),
        P("chan", None),
        P("chan", None),
        P("chan"),
        P("chan"),
    )
    return jax.shard_map(
        local, mesh=mesh, in_specs=in_specs, out_specs=(by_token, by_token), check_vma=False
    )
```

```python
import functools

import jax
import jax.numpy as jnp
import numpy as np
from jax import lax
from jax.experimental import pallas as pl
from jax.experimental.pallas import tpu as pltpu
from jax.sharding import PartitionSpec as P

norm_eps = 1e-06
LANES = 128
MESH = pl.DeviceIdType.MESH
F32 = jnp.float32
BF16 = jnp.bfloat16


def split_table(table):
    high = table.astype(BF16)
    low = (table - high.astype(np.float64)).astype(BF16)
    return high, low


@functools.lru_cache(maxsize=None)
def tables(rows):
    step = np.arange(rows, dtype=np.float64) + 0.5
    outer = 2.0 * np.pi * np.outer(step, step) / (2 * rows)
    inner_at = np.arange(LANES, dtype=np.float64)
    twist = 2.0 * np.pi * np.outer(step, inner_at - LANES / 2) / (2 * rows * LANES)
    inner = 2.0 * np.pi * np.outer(inner_at, inner_at) / LANES
    order = np.concatenate([np.arange(rows // 2), np.arange(rows - 1, rows // 2 - 1, -1)])
    cosine = np.cos(outer)[order]
    halves = [cosine[:, 0::2], cosine[:, 1::2]]
    outer_tab = np.stack([part for half in halves for part in split_table(half)])
    outer_back = np.stack([part for half in halves for part in split_table(half.T)])
    twist_tab = np.stack([np.cos(twist)[order], np.sin(twist)[order]]).astype(np.float32)
    cos, sin = np.cos(inner), np.sin(inner)
    forward = np.block([[cos, -sin], [sin, cos]])
    back = np.block([[cos, sin], [-sin, cos]])
    inner_tab = np.stack([*split_table(forward), *split_table(back)])
    return outer_tab, outer_back, twist_tab, inner_tab


def dot(a, b):
    return jnp.dot(a, b, preferred_element_type=F32)


def iota(shape, dim):
    return lax.broadcasted_iota(jnp.int32, shape, dim)


def main_kernel(
    slots,
    seqo,
    seqi,
    chan,
    index_ref,
    owner_ref,
    skip_ref,
    gate_hbm,
    value_hbm,
    og_hbm,
    res_hbm,
    filt_hbm,
    outer_hbm,
    outback_hbm,
    twist_hbm,
    inner_hbm,
    hid,
    total_ref,
    gate,
    value,
    og,
    res,
    filt,
    outer,
    outback,
    twist,
    inner,
    gated,
    wide,
    wide_og,
    wide_res,
    skip_slot,
    fwide,
    sent,
    arrived,
    fpair,
    spec,
    back,
    ret,
    squares,
    own_sums,
    parts,
    load_sem,
    local_sem,
    send_sem,
    recv_sem,
    bsend_sem,
    brecv_sem,
    zsend_sem,
    zrecv_sem,
):
    owners = seqo * seqi
    pairs = slots // 2
    tok, width = gated.shape
    per = tok // LANES
    rows = per * owners
    live_slots = slots * owners
    me = lax.axis_index("seqo") * seqi + lax.axis_index("seqi")
    mez = lax.axis_index("chan")
    chunks = 4
    crow = tok // chunks

    def load(src, dst, k):
        return pltpu.make_async_copy(src, dst, load_sem.at[k])

    def gate_loads(c):
        at = pl.ds(c * crow, crow)
        return (
            load(gate_hbm.at[at], gate.at[at], 2 * c),
            load(value_hbm.at[at], value.at[at], 2 * c + 1),
        )

    for c in range(chunks):
        for cp in gate_loads(c):
            cp.start()
    nl = 2 * chunks
    filt_load = load(filt_hbm.at[0, 0], filt, nl)
    outer_load = load(outer_hbm, outer, nl + 1)
    twist_load = load(twist_hbm, twist, nl + 2)
    inner_load = load(inner_hbm, inner, nl + 3)
    og_load = load(og_hbm, og, nl + 4)
    res_load = load(res_hbm, res, nl + 5)
    outback_load = load(outback_hbm, outback, nl + 6)
    for cp in (filt_load, outer_load, twist_load, inner_load, outback_load, og_load, res_load):
        cp.start()

    def plane(i):
        o = lax.rem(me + i, owners)
        return o, {"seqo": o // seqi, "seqi": lax.rem(o, seqi)}

    def partner(dy, dx, dc):
        y = lax.rem(lax.axis_index("seqo") + dy, seqo)
        i = lax.axis_index("seqi")
        x = lax.rem(i // 2 + dx, seqi // 2) * 2 + lax.rem(i + dc, 2)
        return y * seqi + x, {"seqo": y, "seqi": x}

    def ring(step, size):
        return min(step, size - step)

    steps = sorted(
        (
            (dy, dx, dc)
            for dy in range(seqo)
            for dx in range(seqi // 2)
            for dc in range(2)
            if dy or dx or dc
        ),
        key=lambda s: -ring(s[0], seqo) - ring(s[1], seqi // 2),
    )

    def column(i):
        return {"chan": lax.rem(mez + i, chan)}

    barrier = pltpu.get_barrier_semaphore()

    for step in steps:
        pl.semaphore_signal(barrier, inc=1, device_id=partner(*step)[1], device_id_type=MESH)
    for i in range(1, chan):
        pl.semaphore_signal(barrier, inc=1, device_id=column(i), device_id_type=MESH)

    kmax = index_ref.shape[1]
    own_row = jnp.broadcast_to(owner_ref[...].astype(F32), (kmax, kmax))
    idx_row = jnp.broadcast_to(index_ref[...].astype(F32), (kmax, kmax))
    sub = iota((kmax, kmax), 0)
    lane = iota((kmax, kmax), 1)
    eye = sub == lane
    own_col = jnp.sum(jnp.where(eye, own_row, 0.0), axis=1, keepdims=True)
    idx_col = jnp.sum(jnp.where(eye, idx_row, 0.0), axis=1, keepdims=True)
    same = (jnp.broadcast_to(own_col, (kmax, kmax)) == own_row) & (sub < lane)
    rank = jnp.sum(jnp.where(same, 1.0, 0.0), axis=0, keepdims=True)
    own_one = owner_ref[...].astype(F32)
    slot_row = jnp.where(own_one >= 0.0, rank * owners + own_one, -1.0)
    slot_at = iota((live_slots, kmax), 0).astype(F32)
    select = jnp.where(slot_at == jnp.broadcast_to(slot_row, (live_slots, kmax)), 1.0, 0.0)
    chan_at = iota((kmax, width), 1).astype(F32)
    spread = jnp.where(chan_at == jnp.broadcast_to(idx_col, (kmax, width)), 1.0, 0.0)
    picker = dot(select.astype(BF16), spread.astype(BF16)).astype(BF16)

    def place(a):
        return a % 2 * (per // 2) + a // 2

    def pick(x):
        return lax.dot_general(picker, x, (((1,), (1,)), ((), ())), preferred_element_type=F32)

    def lay_out(ref, picked, c):
        for q in range(crow // LANES):
            a = place(c * (crow // LANES) + q)
            for r in range(slots):
                ref[r, pl.ds(a, owners, stride=per), :] = picked[
                    r * owners : (r + 1) * owners, q * LANES : (q + 1) * LANES
                ]

    for c in range(chunks):
        for cp in gate_loads(c):
            cp.wait()
        at = pl.ds(c * crow, crow)
        prod = (gate[at].astype(F32) * value[at].astype(F32)).astype(BF16)
        gated[at] = prod
        lay_out(wide, pick(prod), c)

    def span(o):
        return pl.ds(pl.multiple_of(o * per, per), per)

    def exchange(p, src, dst, ssem, rsem):
        mine = pltpu.make_async_copy(
            src.at[p, span(me)], dst.at[p, span(me)], local_sem.at[0]
        )
        mine.start()

        for step in steps:
            o, dev = partner(*step)
            pltpu.make_async_remote_copy(
                src_ref=src.at[p, span(o)],
                dst_ref=dst.at[p, span(me)],
                send_sem=ssem.at[p],
                recv_sem=rsem.at[p],
                device_id=dev,
                device_id_type=MESH,
            ).start()
        mine.wait()

    def whole(p, src, dst, ssem, rsem):
        most = pl.ds(0, rows - per)
        return pltpu.make_async_remote_copy(
            src_ref=src.at[p, most],
            dst_ref=dst.at[p, most],
            send_sem=ssem.at[p],
            recv_sem=rsem.at[p],
            device_id=plane(1)[1],
            device_id_type=MESH,
        )

    for p in range(pairs):
        for ch in range(2):
            sent[p, :, ch * LANES : (ch + 1) * LANES] = wide[2 * p + ch].astype(BF16)
        if p == 0:
            pl.semaphore_wait(barrier, owners + chan - 2)
        exchange(p, sent, arrived, send_sem, recv_sem)

    filt_load.wait()

    half = rows // 2

    def unfold(m, carry):
        taps = filt[:, pl.ds(pl.multiple_of(m * 8 * LANES, 8 * LANES), 8 * LANES)].astype(F32)
        for i in range(8):
            at = pl.ds(i % 2 * half + i // 2 + 4 * m, slots, stride=rows)
            fwide[at, :] = taps[:, i * LANES : (i + 1) * LANES]
        return carry

    lax.fori_loop(0, rows // 8, unfold, 0, unroll=2)
    for r in range(slots):
        fpair[r // 2, :, (r % 2) * LANES : (r % 2 + 1) * LANES] = fwide[
            r * rows : (r + 1) * rows, :
        ].astype(BF16)

    outer_load.wait()
    twist_load.wait()
    inner_load.wait()
    outback_load.wait()

    def parity(x):
        groups = x.astype(F32).reshape(owners, 2, per // 2, 2 * LANES)
        return tuple(groups[:, i].reshape(half, 2 * LANES).astype(BF16) for i in range(2))

    def forward(even, odd):
        low, high = pl.ds(0, half), pl.ds(half, half)
        p = [dot(outer[0, at], even) + dot(outer[1, at], even) for at in (low, high)]
        q = [dot(outer[2, at], odd) + dot(outer[3, at], odd) for at in (low, high)]
        return [
            twisted(at, p[i] + q[i], q[1 - i] - p[1 - i]) for i, at in enumerate((low, high))
        ]

    def twisted(at, re, im):
        tc, ts = twist[0, at], twist[1, at]
        out = []
        for ch in range(2):
            cut = slice(ch * LANES, (ch + 1) * LANES)
            r, m = re[:, cut], im[:, cut]
            z = jnp.concatenate([r * tc + m * ts, m * tc - r * ts], axis=1).astype(BF16)
            out.append(dot(z, inner[0]) + dot(z, inner[1]))
        return out

    scale = 1.0 / (rows * LANES)

    def filter_pair(p, carry):
        got = forward(fpair[p, pl.ds(0, half)], fpair[p, pl.ds(half, half)])
        for i in range(2):
            for ch in range(2):
                spec[2 * p + ch, pl.ds(i * half, half)] = got[i][ch] * scale
        return carry

    lax.fori_loop(0, pairs, filter_pair, 0)

    def convolve_pair(p, carry):
        whole(p, sent, arrived, send_sem, recv_sem).wait_recv()
        got = forward(*parity(arrived[p]))
        turns = []
        for i in range(2):
            at = pl.ds(i * half, half)
            tc, ts = twist[0, at], twist[1, at]
            us, vs = [], []
            for ch in range(2):
                kern = spec[2 * p + ch, at]
                sr, si = got[i][ch][:, :LANES], got[i][ch][:, LANES:]
                kr, ki = kern[:, :LANES], kern[:, LANES:]
                joint = jnp.concatenate([sr * kr - si * ki, sr * ki + si * kr], axis=1)
                joint = joint.astype(BF16)
                u = dot(joint, inner[2]) + dot(joint, inner[3])
                ur, ui = u[:, :LANES], u[:, LANES:]
                us.append(ur * tc - ui * ts)
                vs.append(ui * tc + ur * ts)
            turns.append((jnp.concatenate(us, axis=1), jnp.concatenate(vs, axis=1)))
        halves = []
        for parity_at, sign in ((0, -1.0), (1, 1.0)):
            y = None
            for i in range(2):
                at = slice(i * half, (i + 1) * half)
                w = (turns[i][0] + sign * turns[1 - i][1]).astype(BF16)
                term = dot(outback[2 * parity_at, :, at], w) + dot(outback[2 * parity_at + 1, :, at], w)
                y = term if y is None else y + term
            halves.append(y.reshape(owners, 1, per // 2, 2 * LANES))
        back[p] = jnp.concatenate(halves, axis=1).reshape(rows, 2 * LANES).astype(BF16)
        exchange(p, back, ret, bsend_sem, brecv_sem)
        return carry

    lax.fori_loop(0, pairs, convolve_pair, 0)

    og_load.wait()
    res_load.wait()
    skip = skip_ref[...]
    picker_wide = picker.astype(F32)
    other = jnp.where(jnp.sum(picker_wide, axis=0, keepdims=True) > 0.0, 0.0, 1.0)
    skip_slot[...] = jnp.broadcast_to(
        jnp.sum(picker_wide * skip, axis=1, keepdims=True), skip_slot.shape
    )

    for c in range(chunks):
        at = pl.ds(c * crow, crow)
        lay_out(wide_og, pick(og[at]), c)
        lay_out(wide_res, pick(res[at]), c)

    eye_tile = iota((LANES, LANES), 0) == iota((LANES, LANES), 1)

    def rest_step(a, carry):
        at = pl.ds(pl.multiple_of(a * LANES, LANES), LANES)
        out = res[at].astype(F32) + og[at].astype(F32) * (skip * gated[at].astype(F32))
        out = (out * other).astype(BF16)
        hid[at] = out
        gram = lax.dot_general(out, out, (((1,), (1,)), ((), ())), preferred_element_type=F32)
        line = jnp.where(eye_tile, gram, 0.0)
        squares[pl.ds(place(a), 1), :] = jnp.sum(line, axis=0, keepdims=True)
        return carry

    lax.fori_loop(0, per, rest_step, 0, unroll=2)

    for p in range(pairs):
        whole(p, back, ret, bsend_sem, brecv_sem).wait_recv()
        for ch in range(2):
            r = 2 * p + ch

            def slot_step(o, acc):
                at = pl.ds(pl.multiple_of(o * per, per), per)
                conv = ret[p, at, ch * LANES : (ch + 1) * LANES].astype(F32)
                bias = skip_slot[pl.ds(r * owners + o, 1), :] * wide[r, at]
                h = (wide_res[r, at] + wide_og[r, at] * (conv + bias)).astype(BF16).astype(F32)
                wide[r, at] = h
                return acc + h * h

            squares[...] = lax.fori_loop(0, owners, slot_step, squares[...], unroll=8)

    def send_sums(i):
        pltpu.make_async_remote_copy(
            src_ref=own_sums,
            dst_ref=parts.at[i],
            send_sem=zsend_sem.at[i],
            recv_sem=zrecv_sem.at[i],
            device_id=column(i),
            device_id_type=MESH,
        ).start()

    own_sums[...] = squares[...].astype(BF16)
    for i in (4, 3, 5, 2, 6, 1, 7) if chan == 8 else range(1, chan):
        send_sums(i)

    def final_step(a, carry):
        at = pl.ds(pl.multiple_of(a * LANES, LANES), LANES)
        got = jnp.concatenate(
            [wide[r, pl.ds(place(a), owners, stride=per), :] for r in range(slots)],
            axis=0,
        ).astype(BF16)
        kept = lax.dot_general(got, picker, (((0,), (0,)), ((), ())), preferred_element_type=F32)
        hid[at] = (hid[at].astype(F32) + kept).astype(BF16)
        return carry

    lax.fori_loop(0, per, final_step, 0, unroll=4)

    def take_sums(i, acc):
        cp = pltpu.make_async_remote_copy(
            src_ref=own_sums,
            dst_ref=parts.at[i],
            send_sem=zsend_sem.at[i],
            recv_sem=zrecv_sem.at[i],
            device_id=column(i),
            device_id_type=MESH,
        )
        cp.wait()
        return acc + parts[i].astype(F32)

    total_ref[...] = lax.fori_loop(1, chan, take_sums, own_sums[...].astype(F32))

    for p in range(pairs):
        whole(p, sent, arrived, send_sem, recv_sem).wait_send()
        whole(p, back, ret, bsend_sem, brecv_sem).wait_send()


def norm_kernel(width_all, hid, total_ref, gain_ref, out_hbm, normed_hbm, normed, sem):
    keep = pltpu.make_async_copy(hid, out_hbm, sem.at[0])
    keep.start()
    tok = hid.shape[0]
    eye_tile = iota((LANES, LANES), 0) == iota((LANES, LANES), 1)
    block = 4 * LANES

    def store(b):
        at = pl.ds(b * block, block)
        return pltpu.make_async_copy(normed.at[at], normed_hbm.at[at], sem.at[b + 1])

    for b in range(tok // block):
        for a in range(b * block // LANES, (b + 1) * block // LANES):
            at = pl.ds(a * LANES, LANES)
            row = a % 2 * (tok // LANES // 2) + a // 2
            scaling = lax.rsqrt(total_ref[pl.ds(row, 1), :] / width_all + norm_eps)
            line = jnp.where(eye_tile, jnp.broadcast_to(scaling, (LANES, LANES)), 0.0)
            col = jnp.sum(line, axis=1, keepdims=True)
            normed[at] = (hid[at].astype(F32) * col * gain_ref[...]).astype(BF16)
        store(b).start()
    for b in range(tok // block):
        store(b).wait()
    keep.wait()


def local(
    gate_in, value_in, out_gate, residual, filters, kept_index, kept_owner, skip_bias, norm_gain
):
    tok, width = gate_in.shape
    slots, length = filters.shape[2:]
    seqo, seqi, chan = (lax.axis_size(n) for n in ("seqo", "seqi", "chan"))
    owners = seqo * seqi
    per = tok // LANES
    rows = per * owners
    pairs = slots // 2
    outer_tab, outer_back, twist_tab, inner_tab = tables(rows)
    vmem = pl.BlockSpec(memory_space=pltpu.VMEM)
    hbm = pl.BlockSpec(memory_space=pl.ANY)
    pair_shape = (pairs, rows, 2 * LANES)
    dma = pltpu.SemaphoreType.DMA
    hidden, total = pl.pallas_call(
        functools.partial(main_kernel, slots, seqo, seqi, chan),
        out_shape=(
            pltpu.VMEM((tok, width), BF16),
            pltpu.VMEM((per, LANES), F32),
        ),
        in_specs=[vmem] * 3 + [hbm] * 9,
        out_specs=(vmem, vmem),
        scratch_shapes=[
            pltpu.VMEM((tok, width), BF16),
            pltpu.VMEM((tok, width), BF16),
            pltpu.VMEM((tok, width), BF16),
            pltpu.VMEM((tok, width), BF16),
            pltpu.VMEM((slots, length), BF16),
            pltpu.VMEM(outer_tab.shape, BF16),
            pltpu.VMEM(outer_back.shape, BF16),
            pltpu.VMEM(twist_tab.shape, F32),
            pltpu.VMEM(inner_tab.shape, BF16),
            pltpu.VMEM((tok, width), BF16),
            pltpu.VMEM((slots, rows, LANES), F32),
            pltpu.VMEM((slots, rows, LANES), F32),
            pltpu.VMEM((slots, rows, LANES), F32),
            pltpu.VMEM((slots * owners, LANES), F32),
            pltpu.VMEM((8 * rows, LANES), F32),
            pltpu.VMEM(pair_shape, BF16),
            pltpu.VMEM(pair_shape, BF16),
            pltpu.VMEM(pair_shape, BF16),
            pltpu.VMEM((slots, rows, 2 * LANES), F32),
            pltpu.VMEM(pair_shape, BF16),
            pltpu.VMEM(pair_shape, BF16),
            pltpu.VMEM((per, LANES), F32),
            pltpu.VMEM((per, LANES), BF16),
            pltpu.VMEM((chan, per, LANES), BF16),
            dma((15,)),
            dma((1,)),
            dma((pairs,)),
            dma((pairs,)),
            dma((pairs,)),
            dma((pairs,)),
            dma((chan,)),
            dma((chan,)),
        ],
        compiler_params=pltpu.CompilerParams(
            collective_id=0, has_side_effects=True, vmem_limit_bytes=60 * 1024 * 1024
        ),
        name="hyena",
    )(
        kept_index,
        kept_owner,
        skip_bias.reshape(1, width),
        gate_in,
        value_in,
        out_gate,
        residual,
        filters,
        outer_tab,
        outer_back,
        twist_tab,
        inner_tab,
    )
    return pl.pallas_call(
        functools.partial(norm_kernel, width * chan),
        out_shape=(jax.ShapeDtypeStruct((tok, width), BF16),) * 2,
        in_specs=[vmem] * 3,
        out_specs=(hbm, hbm),
        scratch_shapes=[pltpu.VMEM((tok, width), BF16), dma((tok // (4 * LANES) + 1,))],
        compiler_params=pltpu.CompilerParams(vmem_limit_bytes=8 * 1024 * 1024),
        name="norm",
    )(
        pltpu.with_memory_space_constraint(hidden, pltpu.VMEM),
        pltpu.with_memory_space_constraint(total, pltpu.VMEM),
        norm_gain.reshape(1, width),
    )


def solution(mesh):
    by_token = P(("seqo", "seqi"), "chan")
    in_specs = (
        by_token,
        by_token,
        by_token,
        by_token,
        P("chan", ("seqo", "seqi"), None, None),
        P("chan", None),
        P("chan", None),
        P("chan"),
        P("chan"),
    )
    return jax.shard_map(
        local, mesh=mesh, in_specs=in_specs, out_specs=(by_token, by_token), check_vma=False
    )
```

```python
import functools

import jax
import jax.numpy as jnp
import numpy as np
from jax import lax
from jax.experimental import pallas as pl
from jax.experimental.pallas import tpu as pltpu
from jax.sharding import PartitionSpec as P

norm_eps = 1e-06
LANES = 128
MESH = pl.DeviceIdType.MESH
F32 = jnp.float32
BF16 = jnp.bfloat16


def split_table(table):
    high = table.astype(BF16)
    low = (table - high.astype(np.float64)).astype(BF16)
    return high, low


@functools.lru_cache(maxsize=None)
def tables(rows):
    step = np.arange(rows, dtype=np.float64) + 0.5
    outer = 2.0 * np.pi * np.outer(step, step) / (2 * rows)
    inner_at = np.arange(LANES, dtype=np.float64)
    twist = 2.0 * np.pi * np.outer(step, inner_at - LANES / 2) / (2 * rows * LANES)
    inner = 2.0 * np.pi * np.outer(inner_at, inner_at) / LANES
    order = np.concatenate([np.arange(rows // 2), np.arange(rows - 1, rows // 2 - 1, -1)])
    cosine = np.cos(outer)[order]
    halves = [cosine[:, 0::2], cosine[:, 1::2]]
    outer_tab = np.stack([part for half in halves for part in split_table(half)])
    outer_back = np.stack([part for half in halves for part in split_table(half.T)])
    twist_tab = np.stack([np.cos(twist)[order], np.sin(twist)[order]]).astype(np.float32)
    cos, sin = np.cos(inner), np.sin(inner)
    forward = np.block([[cos, -sin], [sin, cos]])
    back = np.block([[cos, sin], [-sin, cos]])
    inner_tab = np.stack([*split_table(forward), *split_table(back)])
    return outer_tab, outer_back, twist_tab, inner_tab


def dot(a, b):
    return jnp.dot(a, b, preferred_element_type=F32)


def iota(shape, dim):
    return lax.broadcasted_iota(jnp.int32, shape, dim)


def main_kernel(
    slots,
    seqo,
    seqi,
    chan,
    index_ref,
    owner_ref,
    skip_ref,
    gate_hbm,
    value_hbm,
    og_hbm,
    res_hbm,
    filt_hbm,
    outer_hbm,
    outback_hbm,
    twist_hbm,
    inner_hbm,
    hid,
    total_ref,
    gate,
    value,
    og,
    res,
    filt,
    outer,
    outback,
    twist,
    inner,
    gated,
    wide,
    wide_og,
    wide_res,
    skip_slot,
    fwide,
    sent,
    arrived,
    fpair,
    spec,
    back,
    ret,
    squares,
    own_sums,
    parts,
    load_sem,
    local_sem,
    send_sem,
    recv_sem,
    bsend_sem,
    brecv_sem,
    zsend_sem,
    zrecv_sem,
):
    owners = seqo * seqi
    pairs = slots // 2
    tok, width = gated.shape
    per = tok // LANES
    rows = per * owners
    live_slots = slots * owners
    me = lax.axis_index("seqo") * seqi + lax.axis_index("seqi")
    mez = lax.axis_index("chan")
    chunks = 4
    crow = tok // chunks

    def plane(i):
        o = lax.rem(me + i, owners)
        return o, {"seqo": o // seqi, "seqi": lax.rem(o, seqi)}

    def partner(dy, dx, dc):
        y = lax.rem(lax.axis_index("seqo") + dy, seqo)
        i = lax.axis_index("seqi")
        x = lax.rem(i // 2 + dx, seqi // 2) * 2 + lax.rem(i + dc, 2)
        return y * seqi + x, {"seqo": y, "seqi": x}

    def ring(step, size):
        return min(step, size - step)

    steps = sorted(
        (
            (dy, dx, dc)
            for dy in range(seqo)
            for dx in range(seqi // 2)
            for dc in range(2)
            if dy or dx or dc
        ),
        key=lambda s: -ring(s[0], seqo) - ring(s[1], seqi // 2),
    )

    def column(i):
        return {"chan": lax.rem(mez + i, chan)}

    barrier = pltpu.get_barrier_semaphore()

    greets = [(-ring(s[0], seqo) - ring(s[1], seqi // 2), partner, s) for s in steps]
    greets += [(-ring(i, chan), lambda i: (i, column(i)), (i,)) for i in range(1, chan)]
    for _, whom, step in sorted(greets, key=lambda g: g[0]):
        pl.semaphore_signal(barrier, inc=1, device_id=whom(*step)[1], device_id_type=MESH)

    def load(src, dst, k):
        return pltpu.make_async_copy(src, dst, load_sem.at[k])

    def gate_loads(c):
        at = pl.ds(c * crow, crow)
        return (
            load(gate_hbm.at[at], gate.at[at], 2 * c),
            load(value_hbm.at[at], value.at[at], 2 * c + 1),
        )

    for c in range(chunks):
        for cp in gate_loads(c):
            cp.start()
    nl = 2 * chunks
    filt_load = load(filt_hbm.at[0, 0], filt, nl)
    outer_load = load(outer_hbm, outer, nl + 1)
    twist_load = load(twist_hbm, twist, nl + 2)
    inner_load = load(inner_hbm, inner, nl + 3)
    og_load = load(og_hbm, og, nl + 4)
    res_load = load(res_hbm, res, nl + 5)
    outback_load = load(outback_hbm, outback, nl + 6)
    for cp in (filt_load, outer_load, twist_load, inner_load, outback_load, og_load, res_load):
        cp.start()

    kmax = index_ref.shape[1]
    own_row = jnp.broadcast_to(owner_ref[...].astype(F32), (kmax, kmax))
    idx_row = jnp.broadcast_to(index_ref[...].astype(F32), (kmax, kmax))
    sub = iota((kmax, kmax), 0)
    lane = iota((kmax, kmax), 1)
    eye = sub == lane
    own_col = jnp.sum(jnp.where(eye, own_row, 0.0), axis=1, keepdims=True)
    idx_col = jnp.sum(jnp.where(eye, idx_row, 0.0), axis=1, keepdims=True)
    same = (jnp.broadcast_to(own_col, (kmax, kmax)) == own_row) & (sub < lane)
    rank = jnp.sum(jnp.where(same, 1.0, 0.0), axis=0, keepdims=True)
    own_one = owner_ref[...].astype(F32)
    slot_row = jnp.where(own_one >= 0.0, rank * owners + own_one, -1.0)
    slot_at = iota((live_slots, kmax), 0).astype(F32)
    select = jnp.where(slot_at == jnp.broadcast_to(slot_row, (live_slots, kmax)), 1.0, 0.0)
    chan_at = iota((kmax, width), 1).astype(F32)
    spread = jnp.where(chan_at == jnp.broadcast_to(idx_col, (kmax, width)), 1.0, 0.0)
    picker = dot(select.astype(BF16), spread.astype(BF16)).astype(BF16)

    def place(a):
        return a % 2 * (per // 2) + a // 2

    def pick(x):
        return lax.dot_general(picker, x, (((1,), (1,)), ((), ())), preferred_element_type=F32)

    def lay_out(ref, picked, c):
        for q in range(crow // LANES):
            a = place(c * (crow // LANES) + q)
            for r in range(slots):
                ref[r, pl.ds(a, owners, stride=per), :] = picked[
                    r * owners : (r + 1) * owners, q * LANES : (q + 1) * LANES
                ]

    for c in range(chunks):
        for cp in gate_loads(c):
            cp.wait()
        at = pl.ds(c * crow, crow)
        prod = (gate[at].astype(F32) * value[at].astype(F32)).astype(BF16)
        gated[at] = prod
        lay_out(wide, pick(prod), c)

    def span(o):
        return pl.ds(pl.multiple_of(o * per, per), per)

    def exchange(p, src, dst, ssem, rsem):
        mine = pltpu.make_async_copy(
            src.at[p, span(me)], dst.at[p, span(me)], local_sem.at[0]
        )
        mine.start()

        for step in steps:
            o, dev = partner(*step)
            pltpu.make_async_remote_copy(
                src_ref=src.at[p, span(o)],
                dst_ref=dst.at[p, span(me)],
                send_sem=ssem.at[p],
                recv_sem=rsem.at[p],
                device_id=dev,
                device_id_type=MESH,
            ).start()
        mine.wait()

    def whole(p, src, dst, ssem, rsem):
        most = pl.ds(0, rows - per)
        return pltpu.make_async_remote_copy(
            src_ref=src.at[p, most],
            dst_ref=dst.at[p, most],
            send_sem=ssem.at[p],
            recv_sem=rsem.at[p],
            device_id=plane(1)[1],
            device_id_type=MESH,
        )

    for p in range(pairs):
        for ch in range(2):
            sent[p, :, ch * LANES : (ch + 1) * LANES] = wide[2 * p + ch].astype(BF16)
        if p == 0:
            pl.semaphore_wait(barrier, owners + chan - 2)
        exchange(p, sent, arrived, send_sem, recv_sem)

    filt_load.wait()

    half = rows // 2

    def unfold(m, carry):
        taps = filt[:, pl.ds(pl.multiple_of(m * 8 * LANES, 8 * LANES), 8 * LANES)].astype(F32)
        for i in range(8):
            at = pl.ds(i % 2 * half + i // 2 + 4 * m, slots, stride=rows)
            fwide[at, :] = taps[:, i * LANES : (i + 1) * LANES]
        return carry

    lax.fori_loop(0, rows // 8, unfold, 0, unroll=2)
    for r in range(slots):
        fpair[r // 2, :, (r % 2) * LANES : (r % 2 + 1) * LANES] = fwide[
            r * rows : (r + 1) * rows, :
        ].astype(BF16)

    outer_load.wait()
    twist_load.wait()
    inner_load.wait()
    outback_load.wait()

    def parity(x):
        groups = x.astype(F32).reshape(owners, 2, per // 2, 2 * LANES)
        return tuple(groups[:, i].reshape(half, 2 * LANES).astype(BF16) for i in range(2))

    def forward(even, odd):
        low, high = pl.ds(0, half), pl.ds(half, half)
        p = [dot(outer[0, at], even) + dot(outer[1, at], even) for at in (low, high)]
        q = [dot(outer[2, at], odd) + dot(outer[3, at], odd) for at in (low, high)]
        return [
            twisted(at, p[i] + q[i], q[1 - i] - p[1 - i]) for i, at in enumerate((low, high))
        ]

    def twisted(at, re, im):
        tc, ts = twist[0, at], twist[1, at]
        out = []
        for ch in range(2):
            cut = slice(ch * LANES, (ch + 1) * LANES)
            r, m = re[:, cut], im[:, cut]
            z = jnp.concatenate([r * tc + m * ts, m * tc - r * ts], axis=1).astype(BF16)
            out.append(dot(z, inner[0]) + dot(z, inner[1]))
        return out

    scale = 1.0 / (rows * LANES)

    def filter_pair(p, carry):
        got = forward(fpair[p, pl.ds(0, half)], fpair[p, pl.ds(half, half)])
        for i in range(2):
            for ch in range(2):
                spec[2 * p + ch, pl.ds(i * half, half)] = got[i][ch] * scale
        return carry

    lax.fori_loop(0, pairs, filter_pair, 0)

    def convolve_pair(p, carry):
        whole(p, sent, arrived, send_sem, recv_sem).wait_recv()
        got = forward(*parity(arrived[p]))
        turns = []
        for i in range(2):
            at = pl.ds(i * half, half)
            tc, ts = twist[0, at], twist[1, at]
            us, vs = [], []
            for ch in range(2):
                kern = spec[2 * p + ch, at]
                sr, si = got[i][ch][:, :LANES], got[i][ch][:, LANES:]
                kr, ki = kern[:, :LANES], kern[:, LANES:]
                joint = jnp.concatenate([sr * kr - si * ki, sr * ki + si * kr], axis=1)
                joint = joint.astype(BF16)
                u = dot(joint, inner[2]) + dot(joint, inner[3])
                ur, ui = u[:, :LANES], u[:, LANES:]
                us.append(ur * tc - ui * ts)
                vs.append(ui * tc + ur * ts)
            turns.append((jnp.concatenate(us, axis=1), jnp.concatenate(vs, axis=1)))
        halves = []
        for parity_at, sign in ((0, -1.0), (1, 1.0)):
            y = None
            for i in range(2):
                at = slice(i * half, (i + 1) * half)
                w = (turns[i][0] + sign * turns[1 - i][1]).astype(BF16)
                term = dot(outback[2 * parity_at, :, at], w) + dot(outback[2 * parity_at + 1, :, at], w)
                y = term if y is None else y + term
            halves.append(y.reshape(owners, 1, per // 2, 2 * LANES))
        back[p] = jnp.concatenate(halves, axis=1).reshape(rows, 2 * LANES).astype(BF16)
        exchange(p, back, ret, bsend_sem, brecv_sem)
        return carry

    lax.fori_loop(0, pairs, convolve_pair, 0)

    og_load.wait()
    res_load.wait()
    skip = skip_ref[...]
    picker_wide = picker.astype(F32)
    other = jnp.where(jnp.sum(picker_wide, axis=0, keepdims=True) > 0.0, 0.0, 1.0)
    skip_slot[...] = jnp.broadcast_to(
        jnp.sum(picker_wide * skip, axis=1, keepdims=True), skip_slot.shape
    )

    for c in range(chunks):
        at = pl.ds(c * crow, crow)
        lay_out(wide_og, pick(og[at]), c)
        lay_out(wide_res, pick(res[at]), c)

    eye_tile = iota((LANES, LANES), 0) == iota((LANES, LANES), 1)

    def rest_step(a, carry):
        at = pl.ds(pl.multiple_of(a * LANES, LANES), LANES)
        out = res[at].astype(F32) + og[at].astype(F32) * (skip * gated[at].astype(F32))
        out = (out * other).astype(BF16)
        hid[at] = out
        gram = lax.dot_general(out, out, (((1,), (1,)), ((), ())), preferred_element_type=F32)
        line = jnp.where(eye_tile, gram, 0.0)
        squares[pl.ds(place(a), 1), :] = jnp.sum(line, axis=0, keepdims=True)
        return carry

    lax.fori_loop(0, per, rest_step, 0, unroll=2)

    for p in range(pairs):
        whole(p, back, ret, bsend_sem, brecv_sem).wait_recv()
        for ch in range(2):
            r = 2 * p + ch

            def slot_step(o, acc):
                at = pl.ds(pl.multiple_of(o * per, per), per)
                conv = ret[p, at, ch * LANES : (ch + 1) * LANES].astype(F32)
                bias = skip_slot[pl.ds(r * owners + o, 1), :] * wide[r, at]
                h = (wide_res[r, at] + wide_og[r, at] * (conv + bias)).astype(BF16).astype(F32)
                wide[r, at] = h
                return acc + h * h

            squares[...] = lax.fori_loop(0, owners, slot_step, squares[...], unroll=8)

    def send_sums(i):
        pltpu.make_async_remote_copy(
            src_ref=own_sums,
            dst_ref=parts.at[i],
            send_sem=zsend_sem.at[i],
            recv_sem=zrecv_sem.at[i],
            device_id=column(i),
            device_id_type=MESH,
        ).start()

    own_sums[...] = squares[...].astype(BF16)
    for i in (4, 3, 5, 2, 6, 1, 7) if chan == 8 else range(1, chan):
        send_sums(i)

    def final_step(a, carry):
        at = pl.ds(pl.multiple_of(a * LANES, LANES), LANES)
        got = jnp.concatenate(
            [wide[r, pl.ds(place(a), owners, stride=per), :] for r in range(slots)],
            axis=0,
        ).astype(BF16)
        kept = lax.dot_general(got, picker, (((0,), (0,)), ((), ())), preferred_element_type=F32)
        hid[at] = (hid[at].astype(F32) + kept).astype(BF16)
        return carry

    lax.fori_loop(0, per, final_step, 0, unroll=4)

    def take_sums(i, acc):
        cp = pltpu.make_async_remote_copy(
            src_ref=own_sums,
            dst_ref=parts.at[i],
            send_sem=zsend_sem.at[i],
            recv_sem=zrecv_sem.at[i],
            device_id=column(i),
            device_id_type=MESH,
        )
        cp.wait()
        return acc + parts[i].astype(F32)

    total_ref[...] = lax.fori_loop(1, chan, take_sums, own_sums[...].astype(F32))

    for p in range(pairs):
        whole(p, sent, arrived, send_sem, recv_sem).wait_send()
        whole(p, back, ret, bsend_sem, brecv_sem).wait_send()


def norm_kernel(width_all, hid, total_ref, gain_ref, out_hbm, normed_hbm, normed, sem):
    keep = pltpu.make_async_copy(hid, out_hbm, sem.at[0])
    keep.start()
    tok = hid.shape[0]
    eye_tile = iota((LANES, LANES), 0) == iota((LANES, LANES), 1)
    block = 4 * LANES

    def store(b):
        at = pl.ds(b * block, block)
        return pltpu.make_async_copy(normed.at[at], normed_hbm.at[at], sem.at[b + 1])

    for b in range(tok // block):
        for a in range(b * block // LANES, (b + 1) * block // LANES):
            at = pl.ds(a * LANES, LANES)
            row = a % 2 * (tok // LANES // 2) + a // 2
            scaling = lax.rsqrt(total_ref[pl.ds(row, 1), :] / width_all + norm_eps)
            line = jnp.where(eye_tile, jnp.broadcast_to(scaling, (LANES, LANES)), 0.0)
            col = jnp.sum(line, axis=1, keepdims=True)
            normed[at] = (hid[at].astype(F32) * col * gain_ref[...]).astype(BF16)
        store(b).start()
    for b in range(tok // block):
        store(b).wait()
    keep.wait()


def local(
    gate_in, value_in, out_gate, residual, filters, kept_index, kept_owner, skip_bias, norm_gain
):
    tok, width = gate_in.shape
    slots, length = filters.shape[2:]
    seqo, seqi, chan = (lax.axis_size(n) for n in ("seqo", "seqi", "chan"))
    owners = seqo * seqi
    per = tok // LANES
    rows = per * owners
    pairs = slots // 2
    outer_tab, outer_back, twist_tab, inner_tab = tables(rows)
    vmem = pl.BlockSpec(memory_space=pltpu.VMEM)
    hbm = pl.BlockSpec(memory_space=pl.ANY)
    pair_shape = (pairs, rows, 2 * LANES)
    dma = pltpu.SemaphoreType.DMA
    hidden, total = pl.pallas_call(
        functools.partial(main_kernel, slots, seqo, seqi, chan),
        out_shape=(
            pltpu.VMEM((tok, width), BF16),
            pltpu.VMEM((per, LANES), F32),
        ),
        in_specs=[vmem] * 3 + [hbm] * 9,
        out_specs=(vmem, vmem),
        scratch_shapes=[
            pltpu.VMEM((tok, width), BF16),
            pltpu.VMEM((tok, width), BF16),
            pltpu.VMEM((tok, width), BF16),
            pltpu.VMEM((tok, width), BF16),
            pltpu.VMEM((slots, length), BF16),
            pltpu.VMEM(outer_tab.shape, BF16),
            pltpu.VMEM(outer_back.shape, BF16),
            pltpu.VMEM(twist_tab.shape, F32),
            pltpu.VMEM(inner_tab.shape, BF16),
            pltpu.VMEM((tok, width), BF16),
            pltpu.VMEM((slots, rows, LANES), F32),
            pltpu.VMEM((slots, rows, LANES), F32),
            pltpu.VMEM((slots, rows, LANES), F32),
            pltpu.VMEM((slots * owners, LANES), F32),
            pltpu.VMEM((8 * rows, LANES), F32),
            pltpu.VMEM(pair_shape, BF16),
            pltpu.VMEM(pair_shape, BF16),
            pltpu.VMEM(pair_shape, BF16),
            pltpu.VMEM((slots, rows, 2 * LANES), F32),
            pltpu.VMEM(pair_shape, BF16),
            pltpu.VMEM(pair_shape, BF16),
            pltpu.VMEM((per, LANES), F32),
            pltpu.VMEM((per, LANES), BF16),
            pltpu.VMEM((chan, per, LANES), BF16),
            dma((15,)),
            dma((1,)),
            dma((pairs,)),
            dma((pairs,)),
            dma((pairs,)),
            dma((pairs,)),
            dma((chan,)),
            dma((chan,)),
        ],
        compiler_params=pltpu.CompilerParams(
            collective_id=0, has_side_effects=True, vmem_limit_bytes=60 * 1024 * 1024
        ),
        name="hyena",
    )(
        kept_index,
        kept_owner,
        skip_bias.reshape(1, width),
        gate_in,
        value_in,
        out_gate,
        residual,
        filters,
        outer_tab,
        outer_back,
        twist_tab,
        inner_tab,
    )
    return pl.pallas_call(
        functools.partial(norm_kernel, width * chan),
        out_shape=(jax.ShapeDtypeStruct((tok, width), BF16),) * 2,
        in_specs=[vmem] * 3,
        out_specs=(hbm, hbm),
        scratch_shapes=[pltpu.VMEM((tok, width), BF16), dma((tok // (4 * LANES) + 1,))],
        compiler_params=pltpu.CompilerParams(vmem_limit_bytes=8 * 1024 * 1024),
        name="norm",
    )(
        pltpu.with_memory_space_constraint(hidden, pltpu.VMEM),
        pltpu.with_memory_space_constraint(total, pltpu.VMEM),
        norm_gain.reshape(1, width),
    )


def solution(mesh):
    by_token = P(("seqo", "seqi"), "chan")
    in_specs = (
        by_token,
        by_token,
        by_token,
        by_token,
        P("chan", ("seqo", "seqi"), None, None),
        P("chan", None),
        P("chan", None),
        P("chan"),
        P("chan"),
    )
    return jax.shard_map(
        local, mesh=mesh, in_specs=in_specs, out_specs=(by_token, by_token), check_vma=False
    )
```
